128 devices in a mesh: gx: 8 (over x_lo, y), gy: 16 (over z, x_hi, core).
Axes of the slice: x: 4 (x_hi: 2, x_lo: 2; x = x_hi * 2 + x_lo), y: 4, z: 4, core: 2. Of those that a mesh axis runs over, the one named last changes fastest.
Arguments:
- node_shift: float32 [2, 512, 8192], P(None, 'gx', 'gy'), may hold values from -1.5 to 1.5
- node_speed: float32 [2, 512, 8192], P(None, 'gx', 'gy'), may hold values from -4 to 4
- damage_initial: int32 [2, 512, 8192], P(None, 'gx', 'gy'), may hold values from 0 to 7
- cohesive_markers: int32 [64, 16], P('gx', 'gy'), may hold values from 0 to 1, as said below
- cell_warmth: float32 [256, 4096], P(('gx', 'gy')), may hold values from 0 to 1
- heat_storage: float32 [256, 4096], P(('gx', 'gy')), may hold values from 0.5 to 2
- surface_transfer: float32 [256, 4096], P(('gx', 'gy')), may hold values from 0.1 to 1
- quench_liquid_heat: float32 [256, 4096], P(('gx', 'gy')), may hold values from 0 to 0.3
Outputs:
- displace_new: float32 [2, 512, 8192], P(None, 'gx', 'gy')
- velocity_new: float32 [2, 512, 8192], P(None, 'gx', 'gy')
- damage: bfloat16 [2, 512, 8192], P(None, 'gx', 'gy')
- warmth_after_solve: float32 [256, 4096], P(('gx', 'gy'))
The draws below stay inside these ranges and needn't reach their ends.
Inputs may be any that keep to these rules, and one draw needn't show every extreme that they name: `cohesive_markers`: within each column, every block of 8 consecutive tile rows starting at a multiple of 8 holds between 1 and 4 ones, and in every draw some block holds exactly 4.
All inputs are finite; a program needn't handle non-finite values.
Results may differ from the reference program's by a relative error of at most 0.001.
Values sent between devices are 32-bit elements; how exact they have to be, the bound alone decides.
No kernel may reach another device: no remote copies, remote signals or barrier semaphores. Data moves between devices by JAX's collectives and lax.ppermute only.
A program may use at most 64 MiB of HBM per device.

```python
import math
import jax
import jax.numpy as jnp
from jax import lax

FX = 64
FY = 512
SR = 8
SEG = 128
SUBSTEPS = 8
ITERS = 4
NXF = 512
NYF = 8192
CELL_HEIGHT_NUM = 256
CELL_WIDTH_NUM = 4096
STRIPS = 8
MOST = 4
N_GX = 8
N_GY = 16


def marker_grid(key):
    block_total = NXF // FX * N_GY
    key_count, key_force, key_order = jax.random.split(jax.random.fold_in(key, 11), 3)
    counts = jax.random.randint(key_count, (block_total,), 1, MOST + 1)
    forced = jax.random.randint(key_force, (), 0, block_total)
    counts = jnp.where(jnp.arange(block_total) == forced, MOST, counts)
    orders = jax.vmap(lambda subkey: jax.random.permutation(subkey, STRIPS))(jax.random.split(key_order, block_total))
    marking = (orders < counts[:, None]).astype(jnp.int32)
    grid_marks = marking.reshape(NXF // FX, N_GY, STRIPS)
    return jnp.transpose(grid_marks, (0, 2, 1)).reshape(NXF // SR, N_GY)


def draw_cohesive_markers(key, part):
    return marker_grid(key)


def draw_damage_initial(key, part):
    key_level, key_keep = jax.random.split(jax.random.fold_in(key, 23))
    levels = jax.random.randint(key_level, (2, NXF, NYF), 0, 8)
    keeping = jax.random.randint(key_keep, (2, NXF, NYF), 0, 4)
    return jnp.where(keeping == 0, levels, 0).astype(jnp.int32)


def draw_node_speed(key, part):
    key_phase, key_rough = jax.random.split(jax.random.fold_in(key, 31))
    phases = jax.random.uniform(key_phase, (4,), jnp.float32)
    rows = jnp.arange(NXF, dtype=jnp.float32)[:, None]
    cols = jnp.arange(NYF, dtype=jnp.float32)[None, :]
    two_pi = 2.0 * math.pi
    amplitude = 1.6
    rough = jnp.clip(0.25 * jax.random.normal(key_rough, (2, NXF, NYF), jnp.float32), -1.0, 1.0)
    along_rows = amplitude * jnp.sin(two_pi * (rows / 32.0 + phases[0])) * (1.0 + 0.5 * jnp.sin(two_pi * (cols / 64.0 + phases[1])))
    along_cols = amplitude * jnp.sin(two_pi * (cols / 32.0 + phases[2])) * (1.0 + 0.5 * jnp.sin(two_pi * (rows / 64.0 + phases[3])))
    return (jnp.stack([along_rows, along_cols]) + rough).astype(jnp.float32)


def draw_heat_storage(key, part):
    marks = marker_grid(key)
    row_tile = 2 * jnp.arange(CELL_HEIGHT_NUM, dtype=jnp.int32) // SR
    col_tile = 2 * jnp.arange(CELL_WIDTH_NUM, dtype=jnp.int32) // FY
    coarse_marks = marks[row_tile][:, col_tile]
    fraction = jax.random.uniform(jax.random.fold_in(key, 41), (CELL_HEIGHT_NUM, CELL_WIDTH_NUM), jnp.float32)
    lower = jnp.where(coarse_marks == 1, math.log(0.5), math.log(1.25))
    upper = jnp.where(coarse_marks == 1, math.log(1.0), math.log(2.0))
    return jnp.exp(lower + (upper - lower) * fraction).astype(jnp.float32)


def shard_levels(stream_key, shape, cuts, smallest, largest):
    gain = 1.0
    for dim, blocks in cuts:
        steps = jax.random.uniform(jax.random.fold_in(jax.random.fold_in(stream_key, 6), dim), (blocks,), jnp.float32, smallest / len(cuts), largest / len(cuts))
        gain = gain * jnp.repeat(jnp.exp(steps), shape[dim] // blocks).reshape((-1,) + (1,) * (len(shape) - 1 - dim))
    return gain


def bell_draw(own_key, extent, width, most, cuts=(), held_as=jnp.bfloat16):
    result = width * jax.random.normal(own_key, extent, jnp.float32)
    if cuts:
        result = result * shard_levels(own_key, extent, cuts, -0.22, 0.18)
    return jnp.clip(result, -most, most).astype(held_as)


def setup_inputs(seed: int = 0) -> dict:
    key_of = jax.random.split(jax.random.key(seed), 9)
    node_shift = bell_draw(key_of[0], (2, NXF, NYF), 0.1, 1.5, ((1, 8), (2, 16)), jnp.float32)
    node_speed = draw_node_speed(jax.random.fold_in(key_of[8], 71), 0)
    damage_initial = draw_damage_initial(jax.random.fold_in(key_of[8], 71), 0)
    cohesive_markers = draw_cohesive_markers(jax.random.fold_in(key_of[8], 71), 0)
    cell_warmth = jnp.clip(1.0 * jax.random.uniform(key_of[4], (CELL_HEIGHT_NUM, CELL_WIDTH_NUM), jnp.float32) ** shard_levels(key_of[4], (CELL_HEIGHT_NUM, CELL_WIDTH_NUM), ((0, 128),), -0.2, 0.2), 0.0, 1.0)
    heat_storage = draw_heat_storage(jax.random.fold_in(key_of[8], 71), 0)
    surface_transfer = jnp.clip(0.1 + 0.9 * jax.random.uniform(key_of[6], (CELL_HEIGHT_NUM, CELL_WIDTH_NUM), jnp.float32) ** shard_levels(key_of[6], (CELL_HEIGHT_NUM, CELL_WIDTH_NUM), ((0, 128),), -0.2, 0.2), 0.1, 1.0)
    quench_liquid_heat = jnp.clip(0.3 * jax.random.uniform(key_of[7], (CELL_HEIGHT_NUM, CELL_WIDTH_NUM), jnp.float32) ** shard_levels(key_of[7], (CELL_HEIGHT_NUM, CELL_WIDTH_NUM), ((0, 128),), -0.2, 0.2), 0.0, 0.3)
    return dict(node_shift=node_shift, node_speed=node_speed, damage_initial=damage_initial, cohesive_markers=cohesive_markers, cell_warmth=cell_warmth, heat_storage=heat_storage, surface_transfer=surface_transfer, quench_liquid_heat=quench_liquid_heat)


STIFFNESS = 1.0
EXPANSION = 0.6
SOFTENING_SCALE = 0.25
TIME_STEP = 0.4
DAMPING = 0.05
HEAT_INCREMENT = 1.0
GAP_GAIN = 0.5


def softening(opening):
    stretch = jnp.maximum(opening, 0.0)
    return 1.0 - jnp.exp(-stretch * stretch / SOFTENING_SCALE)


def edge_masks(row_first, col_first, height_number_all, width_number, total_rows, total_cols):
    row_index = row_first + jnp.arange(height_number_all, dtype=jnp.int32)
    col_index = col_first + jnp.arange(width_number, dtype=jnp.int32)
    in_rows = (row_index >= 0) & (row_index < total_rows)
    in_cols = (col_index >= 0) & (col_index < total_cols)
    present_horizontal = ((row_index >= 1) & (row_index < total_rows))[:, None] & in_cols[None, :]
    present_vertical = in_rows[:, None] & ((col_index >= 1) & (col_index < total_cols))[None, :]
    return present_horizontal.astype(jnp.float32), present_vertical.astype(jnp.float32)


def march_forward(state_tensors, dense_mesh_heat, present_horizontal, present_vertical):
    disp_x, disp_y, vel_x, vel_y, dam_x, dam_y, weight = [state_tensors[number] for number in range(7)]
    average_horizontal = 0.5 * (dense_mesh_heat[1:, :] + dense_mesh_heat[:-1, :])
    open_x = disp_x[1:, :] - disp_x[:-1, :] - EXPANSION * average_horizontal
    shear_x = disp_y[1:, :] - disp_y[:-1, :]
    new_dx = jnp.maximum(dam_x[1:, :], softening(open_x) * weight[1:, :] * present_horizontal[1:, :])
    spring_x = STIFFNESS * (1.0 - new_dx) * present_horizontal[1:, :]
    normal_x = spring_x * open_x
    along_x = spring_x * shear_x
    average_vertical = 0.5 * (dense_mesh_heat[:, 1:] + dense_mesh_heat[:, :-1])
    open_y = disp_y[:, 1:] - disp_y[:, :-1] - EXPANSION * average_vertical
    shear_y = disp_x[:, 1:] - disp_x[:, :-1]
    new_dy = jnp.maximum(dam_y[:, 1:], softening(open_y) * weight[:, 1:] * present_vertical[:, 1:])
    spring_y = STIFFNESS * (1.0 - new_dy) * present_vertical[:, 1:]
    normal_y = spring_y * open_y
    along_y = spring_y * shear_y
    force_x = (normal_x[1:, 1:-1] - normal_x[:-1, 1:-1]) + (along_y[1:-1, 1:] - along_y[1:-1, :-1])
    force_y = (along_x[1:, 1:-1] - along_x[:-1, 1:-1]) + (normal_y[1:-1, 1:] - normal_y[1:-1, :-1])
    inner_vx = vel_x[1:-1, 1:-1]
    inner_vy = vel_y[1:-1, 1:-1]
    next_vx = inner_vx + TIME_STEP * (force_x - DAMPING * inner_vx)
    next_vy = inner_vy + TIME_STEP * (force_y - DAMPING * inner_vy)
    next_ux = disp_x[1:-1, 1:-1] + TIME_STEP * next_vx
    next_uy = disp_y[1:-1, 1:-1] + TIME_STEP * next_vy
    return jnp.stack([next_ux, next_uy, next_vx, next_vy, new_dx[:-1, 1:-1], new_dy[1:-1, :-1], weight[1:-1, 1:-1]])


def widen_upward(padded):
    middle = padded[1:-1]
    even_rows = 0.75 * middle + 0.25 * padded[:-2]
    odd_rows = 0.75 * middle + 0.25 * padded[2:]
    return jnp.stack([even_rows, odd_rows], axis=1).reshape(2 * middle.shape[0], padded.shape[1])


def widen_sideways(padded):
    middle = padded[:, 1:-1]
    even_cols = 0.75 * middle + 0.25 * padded[:, :-2]
    odd_cols = 0.75 * middle + 0.25 * padded[:, 2:]
    return jnp.stack([even_cols, odd_cols], axis=2).reshape(padded.shape[0], 2 * middle.shape[1])


def kernel_table():
    position = jnp.arange(SEG, dtype=jnp.float32)
    return jnp.exp(-4.0 * jnp.abs(position[:, None] - position[None, :]) / SEG) * (2.0 / SEG)


def radiate(values):
    flattened = values.reshape(-1, SEG)
    product = jnp.dot(flattened, kernel_table(), precision=lax.Precision.HIGHEST, preferred_element_type=jnp.float32)
    return product.reshape(values.shape)


def sweep_plate(state_tensors, dense_margin, mask_x, mask_y):
    padded = jnp.pad(state_tensors, ((0, 0), (1, 1), (1, 1)))

    def one_block(block_index):
        first_row = (block_index * FX).astype(jnp.int32)
        piece_rows = lax.dynamic_slice_in_dim(padded, first_row, FX + 2, 1)
        warmth_lines = lax.dynamic_slice_in_dim(dense_margin, first_row, FX + 2, 0)
        rows_x = lax.dynamic_slice_in_dim(mask_x, first_row, FX + 2, 0)
        rows_y = lax.dynamic_slice_in_dim(mask_y, first_row, FX + 2, 0)
        return march_forward(piece_rows, warmth_lines, rows_x, rows_y)

    blocks = lax.map(one_block, jnp.arange(N_GX, dtype=jnp.int32))
    return jnp.moveaxis(blocks, 0, 1).reshape(7, NXF, NYF)


def heat_baseline_check(cell_warmth, heat_storage, surface_transfer, quench_liquid_heat, thermal_impedance):
    heat_conductance = (1.0 + 0.5 * cell_warmth) / (1.0 + thermal_impedance)
    padded_cond = jnp.pad(heat_conductance, 1)
    row_index = jnp.arange(CELL_HEIGHT_NUM, dtype=jnp.int32)[:, None]
    col_index = jnp.arange(CELL_WIDTH_NUM, dtype=jnp.int32)[None, :]
    cond_down = 0.5 * (heat_conductance + padded_cond[:-2, 1:-1]) * (row_index >= 1).astype(jnp.float32)
    cond_up = 0.5 * (heat_conductance + padded_cond[2:, 1:-1]) * (row_index <= CELL_HEIGHT_NUM - 2).astype(jnp.float32)
    cond_left = 0.5 * (heat_conductance + padded_cond[1:-1, :-2]) * (col_index >= 1).astype(jnp.float32)
    cond_right = 0.5 * (heat_conductance + padded_cond[1:-1, 2:]) * (col_index <= CELL_WIDTH_NUM - 2).astype(jnp.float32)
    offsum = cond_down + cond_up + cond_left + cond_right
    diagonal = (heat_storage / HEAT_INCREMENT + surface_transfer) + offsum
    off_ratio = offsum / diagonal
    bound_low = jnp.min(1.0 - off_ratio)
    bound_high = jnp.max(1.0 + off_ratio)

    def laplace_action(field):
        padded = jnp.pad(field, 1)
        return diagonal * field - (cond_down * padded[:-2, 1:-1] + cond_up * padded[2:, 1:-1]
                                   + cond_left * padded[1:-1, :-2] + cond_right * padded[1:-1, 2:])

    center = 0.5 * (bound_high + bound_low)
    spread = 0.5 * (bound_high - bound_low)
    sigma_ratio = center / spread
    rho_now = 1.0 / sigma_ratio
    forcing_entries = heat_storage / HEAT_INCREMENT * cell_warmth + surface_transfer * quench_liquid_heat
    misfit_norm = forcing_entries - laplace_action(cell_warmth)
    direction = misfit_norm / diagonal / center
    answer_state = cell_warmth
    for iteration in range(ITERS):
        answer_state = answer_state + direction
        if iteration + 1 < ITERS:
            misfit_norm = misfit_norm - laplace_action(direction)
            rho_next = 1.0 / (2.0 * sigma_ratio - rho_now)
            direction = rho_next * rho_now * direction + (2.0 * rho_next / spread) * (misfit_norm / diagonal)
            rho_now = rho_next
    return answer_state


def reference(node_shift, node_speed, damage_initial, cohesive_markers, cell_warmth, heat_storage, surface_transfer, quench_liquid_heat):
    weight = jnp.repeat(jnp.repeat(cohesive_markers, SR, axis=0), FY, axis=1).astype(jnp.float32)
    present_horizontal, present_vertical = edge_masks(0, 0, NXF, NYF, NXF, NYF)
    start_damage = damage_initial.astype(jnp.float32) * 0.125 * weight[None]
    state_tensors = jnp.stack([node_shift[0], node_shift[1], node_speed[0], node_speed[1],
                        start_damage[0] * present_horizontal, start_damage[1] * present_vertical, weight])
    dense_mesh_heat = widen_sideways(widen_upward(jnp.pad(cell_warmth, 1, mode="edge")))
    dense_margin = jnp.pad(dense_mesh_heat, 1)
    mask_x, mask_y = edge_masks(-1, -1, NXF + 2, NYF + 2, NXF, NYF)
    for substep in range(SUBSTEPS):
        state_tensors = sweep_plate(state_tensors, dense_margin, mask_x, mask_y)
    gap_sum = state_tensors[4] + state_tensors[5]
    glowing = radiate(gap_sum)
    thermal_impedance = GAP_GAIN * glowing.reshape(CELL_HEIGHT_NUM, 2, CELL_WIDTH_NUM, 2).sum(axis=(1, 3))
    warmth_after_solve = heat_baseline_check(cell_warmth, heat_storage, surface_transfer, quench_liquid_heat, thermal_impedance)
    return state_tensors[0:2], state_tensors[2:4], state_tensors[4:6].astype(jnp.bfloat16), warmth_after_solve
```

```python
import jax
import jax.numpy as jnp
from jax import lax
from jax.experimental import pallas as pl
from jax.experimental.pallas import tpu as pltpu
from jax.sharding import PartitionSpec as P

F32 = jnp.float32
ROWS, COLS = 64, 512
CROWS, CCOLS = 32, 256
GX, GY = 8, 16
HALO = 8
HROW = 16
EROWS = ROWS + 2 * HROW
ECOLS = COLS + 128
WCOLS = CCOLS + 128
HEAT_ROWS = CROWS + 8
SUBSTEPS = 8
SEG = 128
TIME_STEP = 0.4
DAMPING = 0.05
EXPANSION = 0.6
LOG2E = 1.4426950408889634
HI = lax.Precision.HIGHEST
CHUNK = 56
PAYLOAD = 480 + 48 + 24 + 24 + 16


def lanes(shape):
    return lax.broadcasted_iota(jnp.int32, shape, len(shape) - 1)


def sublanes(shape):
    return lax.broadcasted_iota(jnp.int32, shape, len(shape) - 2)


def turn(value, shift, axis):
    size = value.shape[axis]
    shift %= size
    return value if shift == 0 else pltpu.roll(value, shift, axis)


def mark_rows(marks, first, count, width):
    parts = [
        jnp.full((8, width), marks[first // 8 + k, 0].astype(F32), F32) for k in range(count // 8)
    ]
    return jnp.concatenate(parts, axis=0)


def own_tile(f, u, v, d, marks, rows, first_lane):
    row0, count = rows
    window = (pl.ds(row0, count), pl.ds(first_lane, 128))
    if f < 2:
        return u[(f, *window)]
    if f < 4:
        return TIME_STEP * v[(f - 2, *window)]
    weight = mark_rows(marks, row0, count, 128)
    if f < 6:
        return 1.0 - d[(f - 4, *window)].astype(F32) * (0.125 * weight)
    return weight


def pack_kernel(marks, u, v, d, warm, cap, film, bath, out, lines):
    gy = lax.axis_index("gy")
    lines[0:2, :] = warm[...]
    lines[2:4, :] = cap[...] + film[...]
    lines[4:6, :] = film[...] * (bath[...] - warm[...])
    lines[6:8, :] = jnp.zeros((2, GY * CCOLS), F32)
    lane = lanes((8, 128))
    zero = jnp.zeros((32, 128), F32)
    for g in range(GY):
        at = g * CCOLS
        out[g, 0:8, :] = lines[:, at : at + 128]
        out[g, 8:16, :] = lines[:, at + 128 : at + 256]
        if g > 0:
            left = lines[:, at - 128 : at]
        else:
            left = jnp.broadcast_to(lines[:, 0:1], (8, 128))
        if g < GY - 1:
            right = lines[:, at + 256 : at + 384]
        else:
            right = jnp.broadcast_to(lines[:, GY * CCOLS - 1 : GY * CCOLS], (8, 128))
        out[g, 16:24, :] = jnp.where(lane < 64, right, left)
        out[g, 24:CHUNK, :] = zero

    def edge(first_lane, inner):
        wide = lanes((ROWS, 128))
        packed = jnp.zeros((ROWS, 128), F32)
        for f in range(7):
            tile = own_tile(f, u, v, d, marks, (0, ROWS), first_lane)
            moved = turn(tile, 8 * f - inner, 1)
            packed = jnp.where((wide >= 8 * f) & (wide < 8 * f + 8), moved, packed)
        return packed[:32] + turn(packed[32:], 64, 1)

    @pl.when(gy < GY - 1)
    def _():
        out[gy + 1, 24:CHUNK, :] = edge(COLS - 128, 120)

    @pl.when(gy > 0)
    def _():
        out[gy - 1, 24:CHUNK, :] = edge(0, 0)


def side_tile(f, left, right, row0, count):
    if row0 + count <= 32:
        at, inner = row0, 0
    else:
        at, inner = row0 - 32, 64
    lane = lanes((count, 128))
    from_right = turn(right[at : at + count], -(inner + 8 * f), 1)
    from_left = turn(left[at : at + count], 120 - inner - 8 * f, 1)
    return jnp.where(lane < 8, from_right, jnp.where(lane >= 120, from_left, 0.0))


def sides(recv):
    gy = lax.axis_index("gy")
    left = recv[jnp.maximum(gy - 1, 0), 24:CHUNK, :]
    right = recv[jnp.minimum(gy + 1, GY - 1), 24:CHUNK, :]
    return left, right


def weight_tile(marks, left, right, row0, count):
    lane = lanes((count, 128))
    side = side_tile(6, left, right, row0, count)
    own = mark_rows(marks, row0, count, 128)
    return jnp.where((lane < 8) | (lane >= 120), side, own)


def rim_kernel(marks, u, v, d, recv, up, down):
    left, right = sides(recv)
    for out, row0, coarse0, thin0 in ((up, ROWS - HROW, 16, 24), (down, 0, 0, 0)):
        for f in range(6):
            for k in range(5):
                at = (f * 5 + k) * 16
                if k < 4:
                    tile = own_tile(f, u, v, d, marks, (row0, HROW), 128 * k)
                else:
                    tile = side_tile(f, left, right, row0, HROW)
                out[at : at + 16, :] = tile
        for k in range(3):
            for r in range(0, 16, 2):
                g = (coarse0 + r) // 2
                out[480 + 16 * k + r : 482 + 16 * k + r, :] = recv[g, 8 * k : 8 * k + 2, :]
            for r in range(0, 8, 2):
                g = (thin0 + r) // 2
                for a, base in ((1, 528), (2, 552)):
                    out[base + 8 * k + r : base + 8 * k + r + 2, :] = recv[
                        g, 8 * k + 2 * a : 8 * k + 2 * a + 2, :
                    ]
        out[576:592, :] = weight_tile(marks, left, right, row0, HROW)


def plate_kernel(
    marks, u, v, d, recv, above, below,
    shift_out, speed_out, damage_out, resist_out, coarse_out,
    u0, u1, v0, v1, sx, sy, cw, tx, ty, temp, coarse, gap,
):
    gx = lax.axis_index("gx")
    gy = lax.axis_index("gy")
    left, right = sides(recv)
    fields = (u0, u1, v0, v1, sx, sy)
    pad = 8
    for f, ref in enumerate(fields):
        ref[0:pad, :] = jnp.zeros((pad, ECOLS), F32)
        for k in range(5):
            at = (f * 5 + k) * 16
            cols = pl.ds(128 * k, 128)
            ref[pl.ds(pad, HROW), cols] = above[at : at + 16, :]
            ref[pl.ds(pad + HROW + ROWS, HROW), cols] = below[at : at + 16, :]
            if k < 4:
                ref[pl.ds(pad + HROW, ROWS), cols] = own_tile(f, u, v, d, marks, (0, ROWS), 128 * k)
            else:
                for half in (0, 32):
                    ref[pl.ds(pad + HROW + half, 32), cols] = side_tile(f, left, right, half, 32)
    rate = -4.0 * LOG2E
    for base, source in ((0, above), (HROW + ROWS, below)):
        tile = rate * source[576:592, :]
        cw[pl.ds(base, HROW), pl.ds(COLS, 128)] = tile
        cw[pl.ds(base, HROW), pl.ds(0, COLS)] = jnp.broadcast_to(tile[:, 64:65], (HROW, COLS))
    cw[pl.ds(HROW, ROWS), pl.ds(0, COLS)] = rate * mark_rows(marks, 0, ROWS, COLS)
    for half in (0, 32):
        cw[pl.ds(HROW + half, 32), pl.ds(COLS, 128)] = rate * weight_tile(marks, left, right, half, 32)

    for k in range(3):
        cols = pl.ds(128 * k, 128)
        coarse[0, 0:16, cols] = above[480 + 16 * k : 496 + 16 * k, :]
        coarse[0, 48:64, cols] = below[480 + 16 * k : 496 + 16 * k, :]
        for a, base in ((1, 528), (2, 552)):
            coarse[a, 8:16, cols] = above[base + 8 * k : base + 8 * k + 8, :]
            coarse[a, 48:56, cols] = below[base + 8 * k : base + 8 * k + 8, :]
        for g in range(GY):
            for a in range(3):
                coarse[a, 16 + 2 * g : 18 + 2 * g, cols] = recv[g, 8 * k + 2 * a : 8 * k + 2 * a + 2, :]

    @pl.when(gx == 0)
    def _():
        coarse[0, 0:16, :] = jnp.broadcast_to(coarse[0, 16:17, :], (16, WCOLS))
        coarse[1, 8:16, :] = jnp.ones((8, WCOLS), F32)

    @pl.when(gx == GX - 1)
    def _():
        coarse[0, 48:64, :] = jnp.broadcast_to(coarse[0, 47:48, :], (16, WCOLS))
        coarse[1, 48:56, :] = jnp.ones((8, WCOLS), F32)

    coarse_out[...] = coarse[:, 12 : 12 + HEAT_ROWS, :]

    p = sublanes((128, 128))
    q = lanes((128, 128))
    middle = 32 + q // 2
    beside = middle + 2 * (q % 2) - 1
    widen = jnp.where(p == middle, 0.75, 0.0) + jnp.where(p == beside, 0.25, 0.0)
    i = sublanes((EROWS, 64))
    c = lanes((EROWS, 64))
    middle = 8 + i // 2
    beside = middle + 2 * (i % 2) - 1
    raise_ = jnp.where(c == middle, 0.75, 0.0) + jnp.where(c == beside, 0.25, 0.0)
    warm = coarse[0]

    def columns(k):
        window = turn(warm, 32 - 64 * k, 1)[:, 0:128]
        return jnp.dot(window, widen, precision=HI, preferred_element_type=F32)

    lane64 = lanes((64, 128))
    tiles = [columns(k) for k in range(4)]
    tiles.append(jnp.where(lane64 < 64, columns(4), columns(-1)))
    temp[0:pad, :] = jnp.zeros((pad, ECOLS), F32)
    for k in range(5):
        temp[pl.ds(pad, EROWS), pl.ds(128 * k, 128)] = jnp.dot(
            raise_, tiles[k], precision=HI, preferred_element_type=F32
        )
    lane = lanes((8, ECOLS))
    col = gy * COLS + jnp.where(lane < COLS + 64, lane, lane - ECOLS)
    inner_col = (col >= 1) & (col < GY * COLS)
    for b in range(EROWS // 8):
        own = temp[pl.ds(pad + 8 * b, 8), :]
        tx[pl.ds(8 * b, 8), :] = (0.5 * EXPANSION) * (own + temp[pl.ds(pad + 8 * b - 1, 8), :])
        ty[pl.ds(8 * b, 8), :] = (0.5 * EXPANSION) * (own + turn(own, 1, 1))
        row = gx * ROWS - HROW + 8 * b + sublanes((8, ECOLS))
        here = pl.ds(pad + 8 * b, 8)
        sx[here, :] = jnp.where((row >= 1) & (row < GX * ROWS), sx[here, :], 0.0)
        sy[here, :] = jnp.where(inner_col, sy[here, :], 0.0)

    last_row = sublanes((8, ECOLS)) == 7
    keep = 1.0 - TIME_STEP * DAMPING
    push = TIME_STEP * TIME_STEP

    def substep(_, carry):
        next_nx = jnp.zeros((8, ECOLS), F32)
        next_ax = jnp.zeros((8, ECOLS), F32)
        for b in reversed(range(EROWS // 8)):
            here = pl.ds(pad + 8 * b, 8)
            over = pl.ds(pad + 8 * b - 1, 8)
            flat = pl.ds(8 * b, 8)
            a0, a1 = u0[here, :], u1[here, :]
            rate_here = cw[flat, :]
            open_x = a0 - u0[over, :] - tx[flat, :]
            shear_x = a1 - u1[over, :]
            stretch = jnp.maximum(open_x, 0.0)
            spring_x = jnp.minimum(sx[here, :], jnp.exp2(rate_here * (stretch * stretch)))
            sx[here, :] = spring_x
            nx = spring_x * open_x
            ax = spring_x * shear_x
            open_y = a1 - turn(a1, 1, 1) - ty[flat, :]
            shear_y = a0 - turn(a0, 1, 1)
            stretch = jnp.maximum(open_y, 0.0)
            spring_y = jnp.minimum(sy[here, :], jnp.exp2(rate_here * (stretch * stretch)))
            sy[here, :] = spring_y
            ny = spring_y * open_y
            ay = spring_y * shear_y
            roll_nx = turn(nx, -1, 0)
            roll_ax = turn(ax, -1, 0)
            force0 = jnp.where(last_row, next_nx, roll_nx) - nx + (turn(ay, -1, 1) - ay)
            force1 = jnp.where(last_row, next_ax, roll_ax) - ax + (turn(ny, -1, 1) - ny)
            next_nx, next_ax = roll_nx, roll_ax
            b0 = keep * v0[here, :] + push * force0
            b1 = keep * v1[here, :] + push * force1
            v0[here, :] = b0
            v1[here, :] = b1
            u0[here, :] = a0 + b0
            u1[here, :] = a1 + b1
        return carry

    lax.fori_loop(0, SUBSTEPS, substep, 0)

    own = (pl.ds(pad + HROW, ROWS), pl.ds(0, COLS))
    shift_out[0] = u0[own]
    shift_out[1] = u1[own]
    speed_out[0] = v0[own] * (1.0 / TIME_STEP)
    speed_out[1] = v1[own] * (1.0 / TIME_STEP)
    for b in range(10):
        rows = pl.ds(pad + 8 + 8 * b, 8)
        row = gx * ROWS - 8 + 8 * b + sublanes((8, COLS))
        col = gy * COLS + lanes((8, COLS))
        dx = jnp.where(row >= 1, 1.0 - sx[rows, pl.ds(0, COLS)], 0.0)
        dy = jnp.where(col >= 1, 1.0 - sy[rows, pl.ds(0, COLS)], 0.0)
        gap[pl.ds(8 * b, 8), :] = dx + dy
        if 1 <= b < 9:
            damage_out[0, pl.ds(8 * b - 8, 8), :] = dx.astype(jnp.bfloat16)
            damage_out[1, pl.ds(8 * b - 8, 8), :] = dy.astype(jnp.bfloat16)
    p = sublanes((256, 128))
    q = lanes((256, 128))
    place = (p % SEG).astype(F32)
    even = (2 * (q % 64)).astype(F32)
    table = jnp.exp(jnp.abs(place - even) * (-4.0 / SEG)) + jnp.exp(
        jnp.abs(place - even - 1.0) * (-4.0 / SEG)
    )
    table = jnp.where(p // SEG == q // 64, table * (0.5 * 2.0 / SEG), 0.0)
    for k in range(2):
        wide = pl.ds(256 * k, 256)
        a = sublanes((HEAT_ROWS, 2 * HEAT_ROWS))
        c = lanes((HEAT_ROWS, 2 * HEAT_ROWS))
        pool = jnp.where(c // 2 == a, 1.0, 0.0)
        pair = jnp.dot(pool, gap[:, wide], precision=HI, preferred_element_type=F32)
        resist_out[:, pl.ds(128 * k, 128)] = jnp.dot(
            pair, table, precision=HI, preferred_element_type=F32
        )


def conductances(resist, from_left, from_right, coarse):
    gx = lax.axis_index("gx")
    gy = lax.axis_index("gy")
    shape = (HEAT_ROWS, WCOLS)
    lane = lanes((HEAT_ROWS, 128))
    rim = jnp.where(lane < 64, from_right[...], from_left[...])
    wide = jnp.concatenate([resist[...], rim], axis=1)
    warm = coarse[0]
    conduct = (1.0 + 0.5 * warm) / (1.0 + wide)
    row = gx * CROWS - 4 + sublanes(shape)
    lane = lanes(shape)
    col = gy * CCOLS + jnp.where(lane < CCOLS + 64, lane, lane - WCOLS)
    down = jnp.where(
        (row >= 1) & (row < GX * CROWS), 0.5 * (conduct + turn(conduct, 1, 0)), 0.0
    )
    side = jnp.where(
        (col >= 1) & (col < GY * CCOLS), 0.5 * (conduct + turn(conduct, 1, 1)), 0.0
    )
    up = turn(down, -1, 0)
    far = turn(side, -1, 1)
    offsum = down + up + side + far
    return warm, down, up, side, far, offsum, coarse[1] + offsum


def bound_kernel(resist, from_left, from_right, coarse, out):
    parts = conductances(resist, from_left, from_right, coarse)
    ratio = (parts[5] / parts[6])[4 : 4 + CROWS, 0:CCOLS]
    top = jnp.max(ratio, axis=(0, 1), keepdims=True)
    out[...] = jnp.broadcast_to(top[None], (GX, 8, 128))


def solve_kernel(resist, from_left, from_right, coarse, tops, out):
    warm, down, up, side, far, _, diagonal = conductances(resist, from_left, from_right, coarse)
    inverse = 1.0 / diagonal

    def spread(x):
        return (
            down * turn(x, 1, 0) + up * turn(x, -1, 0) + side * turn(x, 1, 1) + far * turn(x, -1, 1)
        ) * inverse

    start = coarse[2] + (
        down * (turn(warm, 1, 0) - warm)
        + up * (turn(warm, -1, 0) - warm)
        + side * (turn(warm, 1, 1) - warm)
        + far * (turn(warm, -1, 1) - warm)
    )
    z = start * inverse
    y = z + spread(z)
    y2 = spread(spread(y))
    top = jnp.max(jnp.max(tops[...], axis=0), axis=(0, 1), keepdims=True)
    line = jnp.broadcast_to(top, (4, CCOLS))
    for g in range(GY):
        out[g, 0:2, :] = y[4 + 2 * g : 6 + 2 * g, 0:CCOLS]
        out[g, 2:4, :] = y2[4 + 2 * g : 6 + 2 * g, 0:CCOLS]
        out[g, 4:8, :] = line


def finish_kernel(recv, warm, out):
    top = jnp.max(recv[0, 4:8, :], axis=(0, 1), keepdims=True)
    for g in range(1, GY):
        top = jnp.maximum(top, jnp.max(recv[g, 4:8, :], axis=(0, 1), keepdims=True))
    square = top * top
    gain = 8.0 / (8.0 - 8.0 * square + square * square)
    near = gain * (1.0 - square)
    for g in range(GY):
        at = pl.ds(CCOLS * g, CCOLS)
        out[:, at] = warm[:, at] + near * recv[g, 0:2, :] + gain * recv[g, 2:4, :]


def vmem(count):
    return [pl.BlockSpec(memory_space=pltpu.VMEM)] * count


MARKS = pl.BlockSpec(memory_space=pltpu.SMEM)
PARAMS = pltpu.CompilerParams(vmem_limit_bytes=32 * 1024 * 1024)


def shaped(*shape, dtype=F32):
    return jax.ShapeDtypeStruct(shape, dtype)


def neighbours(value_up, value_down, axis):
    count = lax.axis_size(axis)
    ahead = [(i, i + 1) for i in range(count - 1)]
    back = [(j, i) for i, j in ahead]
    return lax.ppermute(value_up, axis, ahead), lax.ppermute(value_down, axis, back)


def exchange(value, axis):
    return lax.all_to_all(value, axis, split_axis=0, concat_axis=0, tiled=True)


def per_device(u, v, d, marks, warm, cap, film, bath):
    packed = pl.pallas_call(
        pack_kernel,
        out_shape=shaped(GY, CHUNK, 128),
        in_specs=[MARKS] + vmem(7),
        out_specs=vmem(1)[0],
        scratch_shapes=[pltpu.VMEM((8, GY * CCOLS), F32)],
        compiler_params=PARAMS,
        name="pack",
    )(marks, u, v, d, warm, cap, film, bath)
    recv = exchange(packed, "gy")
    up, down = pl.pallas_call(
        rim_kernel,
        out_shape=(shaped(PAYLOAD, 128), shaped(PAYLOAD, 128)),
        in_specs=[MARKS] + vmem(4),
        out_specs=tuple(vmem(2)),
        compiler_params=PARAMS,
        name="rim",
    )(marks, u, v, d, recv)
    above, below = neighbours(up, down, "gx")
    fine = pltpu.VMEM((EROWS + 8, ECOLS), F32)
    flat = pltpu.VMEM((EROWS, ECOLS), F32)
    shift, speed, damage, resist, coarse = pl.pallas_call(
        plate_kernel,
        out_shape=(
            shaped(2, ROWS, COLS),
            shaped(2, ROWS, COLS),
            shaped(2, ROWS, COLS, dtype=jnp.bfloat16),
            shaped(HEAT_ROWS, CCOLS),
            shaped(3, HEAT_ROWS, WCOLS),
        ),
        in_specs=[MARKS] + vmem(6),
        out_specs=tuple(vmem(5)),
        scratch_shapes=[fine] * 6
        + [flat] * 3
        + [fine, pltpu.VMEM((3, 64, WCOLS), F32), pltpu.VMEM((80, COLS), F32)],
        compiler_params=PARAMS,
        name="plate",
    )(marks, u, v, d, recv, above, below)
    from_left, from_right = neighbours(resist[:, 128:256], resist[:, 0:128], "gy")
    tops = pl.pallas_call(
        bound_kernel,
        out_shape=shaped(GX, 8, 128),
        in_specs=vmem(4),
        out_specs=vmem(1)[0],
        compiler_params=PARAMS,
        name="bound",
    )(resist, from_left, from_right, coarse)
    tops = exchange(tops, "gx")
    answer = pl.pallas_call(
        solve_kernel,
        out_shape=shaped(GY, 8, CCOLS),
        in_specs=vmem(5),
        out_specs=vmem(1)[0],
        compiler_params=PARAMS,
        name="solve",
    )(resist, from_left, from_right, coarse, tops)
    answer = exchange(answer, "gy")
    warmth = pl.pallas_call(
        finish_kernel,
        out_shape=shaped(2, GY * CCOLS),
        in_specs=vmem(2),
        out_specs=vmem(1)[0],
        compiler_params=PARAMS,
        name="finish",
    )(answer, warm)
    return shift, speed, damage, warmth


def solution(mesh):
    tile = P(None, "gx", "gy")
    line = P(("gx", "gy"), None)
    return jax.shard_map(
        per_device,
        mesh=mesh,
        in_specs=(tile, tile, tile, P("gx", "gy"), line, line, line, line),
        out_specs=(tile, tile, tile, line),
        check_vma=False,
    )
```

```python
import jax
import jax.numpy as jnp
from jax import lax
from jax.experimental import pallas as pl
from jax.experimental.pallas import tpu as pltpu
from jax.sharding import PartitionSpec as P

F32 = jnp.float32
ROWS, COLS = 64, 512
CROWS, CCOLS = 32, 256
GX, GY = 8, 16
HALO = 8
HROW = 16
EROWS = ROWS + 2 * HROW
ECOLS = COLS + 128
WCOLS = CCOLS + 128
HEAT_ROWS = CROWS + 8
BAND = EROWS // 8
SUBSTEPS = 8
SEG = 128
TIME_STEP = 0.4
DAMPING = 0.05
EXPANSION = 0.6
LOG2E = 1.4426950408889634
HI = lax.Precision.HIGHEST
CHUNK = 56
CORNER = 16 + 48 + 24 + 24


def lanes(shape):
    return lax.broadcasted_iota(jnp.int32, shape, len(shape) - 1)


def sublanes(shape):
    return lax.broadcasted_iota(jnp.int32, shape, len(shape) - 2)


def turn(value, shift, axis):
    size = value.shape[axis]
    shift %= size
    return value if shift == 0 else pltpu.roll(value, shift, axis)


def mark_rows(marks, first, count, width):
    parts = [
        jnp.full((8, width), marks[first // 8 + k].astype(F32), F32) for k in range(count // 8)
    ]
    return jnp.concatenate(parts, axis=0)


def own_spring(d, marks, f, row0, count, first_lane, width):
    weight = mark_rows(marks, row0, count, width)
    level = d[f, pl.ds(row0, count), pl.ds(first_lane, width)].astype(F32)
    return 1.0 - level * (0.125 * weight)


def start_all(copies):
    for copy in copies:
        copy.start()


def wait_all(copies):
    for copy in copies:
        copy.wait()


def pack_kernel(
    marks, u_hbm, v_hbm, d_hbm, warm_hbm, cap_hbm, film_hbm, bath_hbm,
    out, up, down,
    u, v, d, warm, cap, film, bath, lines, sem,
):
    pairs = (
        (warm_hbm, warm), (cap_hbm, cap), (film_hbm, film), (bath_hbm, bath),
        (u_hbm, u), (v_hbm, v), (d_hbm, d),
    )
    copies = [pltpu.make_async_copy(a, b, sem.at[k]) for k, (a, b) in enumerate(pairs)]
    start_all(copies)
    gy = lax.axis_index("gy")
    zero = jnp.zeros((32, 128), F32)
    for g in range(GY):
        out[g, 24:CHUNK, :] = zero
    wait_all(copies)
    for message, row0 in ((up, ROWS - HROW), (down, 0)):
        rows = pl.ds(row0, HROW)
        for f in range(2):
            for k in range(4):
                cols = pl.ds(128 * k, 128)
                message[f, k] = u[f, rows, cols]
                message[2 + f, k] = v[f, rows, cols]
                message[4 + f, k] = own_spring(d, marks, f, row0, HROW, 128 * k, 128)

    lines[0:2, :] = warm[...]
    lines[2:4, :] = cap[...] + film[...]
    lines[4:6, :] = film[...] * (bath[...] - warm[...])
    lines[6:8, :] = jnp.zeros((2, GY * CCOLS), F32)
    lane = lanes((8, 128))
    for g in range(GY):
        at = g * CCOLS
        out[g, 0:8, :] = lines[:, at : at + 128]
        out[g, 8:16, :] = lines[:, at + 128 : at + 256]
        if g > 0:
            left = lines[:, at - 128 : at]
        else:
            left = jnp.broadcast_to(lines[:, 0:1], (8, 128))
        if g < GY - 1:
            right = lines[:, at + 256 : at + 384]
        else:
            right = jnp.broadcast_to(lines[:, GY * CCOLS - 1 : GY * CCOLS], (8, 128))
        out[g, 16:24, :] = jnp.where(lane < 64, right, left)

    def edge(first_lane, inner):
        wide = lanes((ROWS, 128))
        window = (slice(None), pl.ds(first_lane, 128))
        packed = jnp.zeros((ROWS, 128), F32)
        for f in range(7):
            if f < 2:
                tile = u[(f, *window)]
            elif f < 4:
                tile = v[(f - 2, *window)]
            elif f < 6:
                tile = own_spring(d, marks, f - 4, 0, ROWS, first_lane, 128)
            else:
                tile = mark_rows(marks, 0, ROWS, 128)
            moved = turn(tile, 8 * f - inner, 1)
            packed = jnp.where((wide >= 8 * f) & (wide < 8 * f + 8), moved, packed)
        return packed[:32] + turn(packed[32:], 64, 1)

    @pl.when(gy < GY - 1)
    def _():
        out[gy + 1, 24:CHUNK, :] = edge(COLS - 128, 120)

    @pl.when(gy > 0)
    def _():
        out[gy - 1, 24:CHUNK, :] = edge(0, 0)


def join_sides(f, left, left_at, right, right_at):
    lane = lanes(left.shape)
    from_right = turn(right, -(right_at + 8 * f), 1)
    from_left = turn(left, 120 - left_at - 8 * f, 1)
    return jnp.where(lane < 8, from_right, jnp.where(lane >= 120, from_left, 0.0))


def sides(recv):
    gy = lax.axis_index("gy")
    left = recv[jnp.maximum(gy - 1, 0), 24:CHUNK, :]
    right = recv[jnp.minimum(gy + 1, GY - 1), 24:CHUNK, :]
    return left, right


def rim_kernel(marks, recv, up, down):
    left, right = sides(recv)
    lane = lanes((HROW, 128))
    for out, row0, coarse0, thin0 in ((up, ROWS - HROW, 16, 24), (down, 0, 0, 0)):
        if row0 == 0:
            near, off = left[0:16], turn(right[0:16], 64, 1)
        else:
            near, off = turn(left[16:32], 64, 1), right[16:32]
        corner = jnp.where(lane < 56, near, off)
        out[0:16, :] = jnp.where(
            (lane >= 56) & (lane < 64), mark_rows(marks, row0, HROW, 128), corner
        )
        for k in range(3):
            for r in range(0, 16, 2):
                g = (coarse0 + r) // 2
                out[16 + 16 * k + r : 18 + 16 * k + r, :] = recv[g, 8 * k : 8 * k + 2, :]
            for r in range(0, 8, 2):
                g = (thin0 + r) // 2
                for a, base in ((1, 64), (2, 88)):
                    out[base + 8 * k + r : base + 8 * k + r + 2, :] = recv[
                        g, 8 * k + 2 * a : 8 * k + 2 * a + 2, :
                    ]


def plate_kernel(
    marks, u, v, d, recv, above_rows, below_rows, above, below,
    shift_out, speed_out, damage_out, resist_out, coarse_out, tops_out,
    field, cw, temp, state, rate, warmth, tx, ty, coarse, gap, worn, sem,
):
    gx = lax.axis_index("gx")
    gy = lax.axis_index("gy")
    top = pl.ds(0, HROW)
    mid = pl.ds(HROW, ROWS)
    low = pl.ds(HROW + ROWS, HROW)
    copies = [
        pltpu.make_async_copy(above_rows, field.at[:, 0:4, top], sem.at[0]),
        pltpu.make_async_copy(below_rows, field.at[:, 0:4, low], sem.at[1]),
    ]
    results = []
    for k in range(4):
        cols = pl.ds(128 * k, 128)
        for f, (source, target) in enumerate(((u, shift_out), (v, speed_out))):
            here = field.at[2 * f : 2 * f + 2, k, mid]
            at = 2 + 2 * k + f
            copies.append(pltpu.make_async_copy(source.at[:, :, cols], here, sem.at[at]))
            results.append(pltpu.make_async_copy(here, target.at[:, :, cols], sem.at[8 + at]))
    results.append(pltpu.make_async_copy(worn, damage_out, sem.at[18]))
    start_all(copies)

    for k in range(3):
        cols = pl.ds(128 * k, 128)
        coarse[0, 0:16, cols] = above[16 + 16 * k : 32 + 16 * k, :]
        coarse[0, 48:64, cols] = below[16 + 16 * k : 32 + 16 * k, :]
        for a, base in ((1, 64), (2, 88)):
            coarse[a, 8:16, cols] = above[base + 8 * k : base + 8 * k + 8, :]
            coarse[a, 48:56, cols] = below[base + 8 * k : base + 8 * k + 8, :]
        for g in range(GY):
            for a in range(3):
                coarse[a, 16 + 2 * g : 18 + 2 * g, cols] = recv[g, 8 * k + 2 * a : 8 * k + 2 * a + 2, :]

    @pl.when(gx == 0)
    def _():
        coarse[0, 0:16, :] = jnp.broadcast_to(coarse[0, 16:17, :], (16, WCOLS))
        coarse[1, 8:16, :] = jnp.ones((8, WCOLS), F32)

    @pl.when(gx == GX - 1)
    def _():
        coarse[0, 48:64, :] = jnp.broadcast_to(coarse[0, 47:48, :], (16, WCOLS))
        coarse[1, 48:56, :] = jnp.ones((8, WCOLS), F32)

    coarse_out[...] = coarse[:, 12 : 12 + HEAT_ROWS, :]

    p = sublanes((128, 128))
    q = lanes((128, 128))
    middle = 32 + q // 2
    beside = middle + 2 * (q % 2) - 1
    widen = jnp.where(p == middle, 0.75, 0.0) + jnp.where(p == beside, 0.25, 0.0)
    i = sublanes((EROWS, 64))
    c = lanes((EROWS, 64))
    middle = 8 + i // 2
    beside = middle + 2 * (i % 2) - 1
    raise_ = jnp.where(c == middle, 0.75, 0.0) + jnp.where(c == beside, 0.25, 0.0)
    warm = coarse[0]

    def columns(k):
        window = turn(warm, 32 - 64 * k, 1)[:, 0:128]
        return jnp.dot(window, widen, precision=HI, preferred_element_type=F32)

    lane64 = lanes((64, 128))
    tiles = [columns(k) for k in range(4)]
    tiles.append(jnp.where(lane64 < 64, columns(4), columns(-1)))
    for k in range(5):
        temp[k] = jnp.dot(
            raise_, tiles[k], precision=HI, preferred_element_type=F32
        )

    left, right = sides(recv)
    for f in range(6):
        for rows, source in ((top, above), (low, below)):
            tile = source[0:16, :]
            field[f, 4, rows, :] = join_sides(f, tile, 0, tile, 64)
        for half in (0, 32):
            field[f, 4, pl.ds(HROW + half, 32), :] = join_sides(f, left, half * 2, right, half * 2)
    factor = -4.0 * LOG2E
    for base, source in ((0, above), (HROW + ROWS, below)):
        tile = factor * source[0:16, :]
        cw[1, pl.ds(base, HROW), :] = join_sides(6, tile, 0, tile, 64)
        cw[0, pl.ds(base, HROW), :] = jnp.broadcast_to(tile[:, 60:61], (HROW, 128))
    cw[0, mid, :] = factor * mark_rows(marks, 0, ROWS, 128)
    for half in (0, 32):
        cw[1, pl.ds(HROW + half, 32), :] = factor * join_sides(6, left, half * 2, right, half * 2)
    for f in range(2):
        for k in range(4):
            field[4 + f, k, mid, :] = own_spring(d, marks, f, 0, ROWS, 128 * k, 128)
    wait_all(copies)

    lane = lanes((8, 128))
    first = gx * ROWS - HROW + BAND * sublanes((8, 128))
    for t in range(BAND):
        strip = pl.ds(t, 8, stride=BAND)
        row = first + t
        inner_row = (row >= 1) & (row < GX * ROWS)
        own_rate = cw[0, strip, :]
        side_rate = cw[1, strip, :]
        for k in range(5):
            cols = pl.ds(128 * k, 128)
            rate[t, :, cols] = own_rate if k < 4 else side_rate
            warmth[t, :, cols] = (0.5 * EXPANSION) * temp[k, strip, :]
            for f in range(4):
                state[f, t, :, cols] = field[f, k, strip, :]
            state[4, t, :, cols] = jnp.where(inner_row, field[4, k, strip, :], 0.0)
            spring = field[5, k, strip, :]
            if k in (0, 4):
                col = gy * COLS + (lane if k == 0 else jnp.where(lane < 64, lane + COLS, lane - 128))
                spring = jnp.where((col >= 1) & (col < GY * COLS), spring, 0.0)
            state[5, t, :, cols] = spring
    before = turn(warmth[BAND - 1], 1, 0)
    for t in range(BAND):
        own = warmth[t]
        tx[t] = own + before
        ty[t] = own + turn(own, 1, 1)
        before = own

    keep = 1.0 - TIME_STEP * DAMPING

    def edge_x(t, a0, a1, o0, o1):
        open_x = a0 - o0 - tx[t]
        stretch = jnp.maximum(open_x, 0.0)
        spring = jnp.minimum(state[4, t], jnp.exp2(rate[t] * (stretch * stretch)))
        state[4, t] = spring
        return spring * open_x, spring * (a1 - o1)

    def substep(_, carry):
        a0, a1 = state[0, BAND - 1], state[1, BAND - 1]
        first_nx, first_ax = edge_x(0, state[0, 0], state[1, 0], turn(a0, 1, 0), turn(a1, 1, 0))
        next_nx, next_ax = turn(first_nx, -1, 0), turn(first_ax, -1, 0)
        for t in reversed(range(BAND)):
            open_y = a1 - turn(a1, 1, 1) - ty[t]
            stretch = jnp.maximum(open_y, 0.0)
            spring = jnp.minimum(state[5, t], jnp.exp2(rate[t] * (stretch * stretch)))
            state[5, t] = spring
            ny = spring * open_y
            ay = spring * (a0 - turn(a0, 1, 1))
            if t > 0:
                o0, o1 = state[0, t - 1], state[1, t - 1]
                nx, ax = edge_x(t, a0, a1, o0, o1)
            else:
                o0, o1 = a0, a1
                nx, ax = first_nx, first_ax
            force0 = (next_nx - nx) + (turn(ay, -1, 1) - ay)
            force1 = (next_ax - ax) + (turn(ny, -1, 1) - ny)
            next_nx, next_ax = nx, ax
            b0 = keep * state[2, t] + TIME_STEP * force0
            b1 = keep * state[3, t] + TIME_STEP * force1
            state[2, t] = b0
            state[3, t] = b1
            state[0, t] = a0 + TIME_STEP * b0
            state[1, t] = a1 + TIME_STEP * b1
            a0, a1 = o0, o1
        return carry

    lax.fori_loop(0, SUBSTEPS, substep, 0)
    for f in range(6):
        for t in range(BAND):
            for k in range(4):
                field[f, k, pl.ds(t, 8, stride=BAND), :] = state[f, t, :, pl.ds(128 * k, 128)]
        if f == 3:
            start_all(results[:-1])
    for b in range(10):
        rows = pl.ds(8 + 8 * b, 8)
        row = gx * ROWS - 8 + 8 * b + sublanes((8, 128))
        for k in range(4):
            cols = pl.ds(128 * k, 128)
            dx = jnp.where(row >= 1, 1.0 - field[4, k, rows, :], 0.0)
            dy = 1.0 - field[5, k, rows, :]
            if k == 0:
                dy = jnp.where(gy * COLS + lane >= 1, dy, 0.0)
            gap[pl.ds(8 * b, 8), cols] = dx + dy
            if 1 <= b < 9:
                worn[0, pl.ds(8 * b - 8, 8), cols] = dx.astype(jnp.bfloat16)
                worn[1, pl.ds(8 * b - 8, 8), cols] = dy.astype(jnp.bfloat16)
    start_all(results[-1:])
    p = sublanes((256, 128))
    q = lanes((256, 128))
    place = (p % SEG).astype(F32)
    even = (2 * (q % 64)).astype(F32)
    table = jnp.exp(jnp.abs(place - even) * (-4.0 / SEG)) + jnp.exp(
        jnp.abs(place - even - 1.0) * (-4.0 / SEG)
    )
    table = jnp.where(p // SEG == q // 64, table * (0.5 * 2.0 / SEG), 0.0)
    a = sublanes((HEAT_ROWS, 2 * HEAT_ROWS))
    c = lanes((HEAT_ROWS, 2 * HEAT_ROWS))
    pool = jnp.where(c // 2 == a, 1.0, 0.0)
    for k in range(2):
        pair = jnp.dot(pool, gap[:, pl.ds(256 * k, 256)], precision=HI, preferred_element_type=F32)
        resist_out[:, pl.ds(128 * k, 128)] = jnp.dot(
            pair, table, precision=HI, preferred_element_type=F32
        )
    conduct = (1.0 + 0.5 * coarse[0, 12 : 12 + HEAT_ROWS, 0:CCOLS]) / (1.0 + resist_out[...])
    shape = (HEAT_ROWS, CCOLS)
    row = gx * CROWS - 4 + sublanes(shape)
    down = jnp.where((row >= 1) & (row < GX * CROWS), 0.5 * (conduct + turn(conduct, 1, 0)), 0.0)
    side = jnp.where(lanes(shape) >= 1, 0.5 * (conduct + turn(conduct, 1, 1)), 0.0)
    offsum = (down + turn(down, -1, 0) + side + turn(side, -1, 1))[4 : 4 + CROWS]
    capacity = coarse[1, 16:48, 0:CCOLS]
    top = jnp.max(offsum / (capacity + offsum), axis=(0, 1), keepdims=True)
    a = sublanes((8, CCOLS))
    c = lanes((8, CCOLS))
    border = jnp.where(sublanes((8, 128)) >= 6, top, 0.0)
    for k, value in enumerate((offsum, capacity, conduct[4 : 4 + CROWS])):
        pick = jnp.where(
            ((a == 2 * k) & (c == 0)) | ((a == 2 * k + 1) & (c == CCOLS - 1)), 1.0, 0.0
        )
        border += lax.dot_general(
            pick,
            jnp.concatenate([value] * 4, axis=0),
            (((1,), (1,)), ((), ())),
            precision=HI,
            preferred_element_type=F32,
        )
    for g in range(GX):
        tops_out[g] = border
    wait_all(results)


def conductances(resist, from_left, coarse):
    gx = lax.axis_index("gx")
    gy = lax.axis_index("gy")
    shape = (HEAT_ROWS, WCOLS)
    lane = lanes((HEAT_ROWS, 128))
    rim = jnp.where(lane < 64, 0.0, from_left[...])
    wide = jnp.concatenate([resist[...], rim], axis=1)
    warm = coarse[0]
    conduct = (1.0 + 0.5 * warm) / (1.0 + wide)
    row = gx * CROWS - 4 + sublanes(shape)
    lane = lanes(shape)
    col = gy * CCOLS + jnp.where(lane < CCOLS + 64, lane, lane - WCOLS)
    down = jnp.where(
        (row >= 1) & (row < GX * CROWS), 0.5 * (conduct + turn(conduct, 1, 0)), 0.0
    )
    side = jnp.where(
        (col >= 1) & (col < GY * CCOLS), 0.5 * (conduct + turn(conduct, 1, 1)), 0.0
    )
    up = turn(down, -1, 0)
    far = turn(side, -1, 1)
    offsum = down + up + side + far
    return warm, down, up, side, far, offsum, coarse[1] + offsum


def solve_kernel(resist, from_left, coarse, tops, out):
    warm, down, up, side, far, _, diagonal = conductances(resist, from_left, coarse)
    inverse = 1.0 / diagonal

    def spread(x):
        return (
            down * turn(x, 1, 0) + up * turn(x, -1, 0) + side * turn(x, 1, 1) + far * turn(x, -1, 1)
        ) * inverse

    start = coarse[2] + (
        down * (turn(warm, 1, 0) - warm)
        + up * (turn(warm, -1, 0) - warm)
        + side * (turn(warm, 1, 1) - warm)
        + far * (turn(warm, -1, 1) - warm)
    )
    z = start * inverse
    y = z + spread(z)
    y2 = turn(spread(spread(y)), 4, 1)
    y = turn(y, 4, 1)
    group = lanes((8, 128)) // 32
    strip = []
    for h in range(2):
        tile = tops[4 * h]
        for k in range(1, 4):
            tile = jnp.where(group == k, tops[4 * h + k], tile)
        strip.append(tile)
    for g in range(GY):
        rows = slice(4 + 2 * g, 6 + 2 * g)
        out[g, 0:2, :] = y[rows, 0:CCOLS]
        out[g, 2:4, :] = y2[rows, 0:CCOLS]
        out[g, 4:6, 0:128] = y[rows, CCOLS:]
        out[g, 4:6, 128:256] = y2[rows, CCOLS:]
        out[g, 8:16, 0:128] = strip[0]
        out[g, 8:16, 128:256] = strip[1]


def finish_kernel(recv, warm, out, wide, border):
    for g in range(GY):
        for k in range(7):
            border[k, g : g + 1, :] = recv[g, 8 + k : 9 + k, :]
    across = 0.5 * (turn(border[5], 1, 0) + border[4])
    across = jnp.where(sublanes((GY, CCOLS)) >= 1, across, 0.0)
    top = border[6]
    for k, face in ((0, across), (1, turn(across, -1, 0))):
        offsum = border[k] + face
        top = jnp.maximum(top, offsum / (border[2 + k] + offsum))
    top = jnp.max(top, axis=(0, 1), keepdims=True)
    square = top * top
    gain = 8.0 / (8.0 - 8.0 * square + square * square)
    near = gain * (1.0 - square)
    for g in range(GY):
        wide[:, pl.ds(CCOLS * g, CCOLS)] = near * recv[g, 0:2, :] + gain * recv[g, 2:4, :]
    wide[:, pl.ds(CCOLS * GY, 128)] = (
        near * recv[GY - 1, 4:6, 0:128] + gain * recv[GY - 1, 4:6, 128:256]
    )
    out[...] = warm[...] + turn(wide[...], -4, 1)[:, : GY * CCOLS]


def vmem(count):
    return [pl.BlockSpec(memory_space=pltpu.VMEM)] * count


MARKS = pl.BlockSpec(memory_space=pltpu.SMEM)
ANY = pl.BlockSpec(memory_space=pl.ANY)
FAR = pl.BlockSpec(memory_space=pltpu.MemorySpace.HBM)
PARAMS = pltpu.CompilerParams(vmem_limit_bytes=32 * 1024 * 1024)
ALL_ROOM = pltpu.CompilerParams(vmem_limit_bytes=63 * 1024 * 1024)


def shaped(*shape, dtype=F32):
    return jax.ShapeDtypeStruct(shape, dtype)


def ahead(axis):
    return [(i, i + 1) for i in range(lax.axis_size(axis) - 1)]


def neighbours(value_up, value_down, axis):
    back = [(j, i) for i, j in ahead(axis)]
    return lax.ppermute(value_up, axis, ahead(axis)), lax.ppermute(value_down, axis, back)


def exchange(value, axis):
    return lax.all_to_all(value, axis, split_axis=0, concat_axis=0, tiled=True)


def per_device(u, v, d, marks, warm, cap, film, bath):
    marks = marks.reshape(ROWS // 8)
    tile = pltpu.VMEM((2, ROWS, COLS), F32)
    line = pltpu.VMEM((2, GY * CCOLS), F32)
    packed, up_rows, down_rows = pl.pallas_call(
        pack_kernel,
        out_shape=(shaped(GY, CHUNK, 128), shaped(6, 4, HROW, 128), shaped(6, 4, HROW, 128)),
        in_specs=[MARKS] + [FAR] * 7,
        out_specs=tuple(vmem(3)),
        scratch_shapes=[tile, tile, pltpu.VMEM((2, ROWS, COLS), jnp.int32)]
        + [line] * 4
        + [pltpu.VMEM((8, GY * CCOLS), F32), pltpu.SemaphoreType.DMA((7,))],
        compiler_params=ALL_ROOM,
        name="pack",
    )(marks, u, v, d, warm, cap, film, bath)
    above_rows, below_rows = neighbours(up_rows, down_rows, "gx")
    recv = exchange(packed, "gy")
    up, down = pl.pallas_call(
        rim_kernel,
        out_shape=(shaped(CORNER, 128), shaped(CORNER, 128)),
        in_specs=[MARKS] + vmem(1),
        out_specs=tuple(vmem(2)),
        compiler_params=PARAMS,
        name="rim",
    )(marks, recv)
    above, below = neighbours(up, down, "gx")
    band = pltpu.VMEM((BAND, 8, ECOLS), F32)
    shift, speed, damage, resist, coarse, tops = pl.pallas_call(
        plate_kernel,
        out_shape=(
            shaped(2, ROWS, COLS),
            shaped(2, ROWS, COLS),
            shaped(2, ROWS, COLS, dtype=jnp.bfloat16),
            shaped(HEAT_ROWS, CCOLS),
            shaped(3, HEAT_ROWS, WCOLS),
            shaped(GX, 8, 128),
        ),
        in_specs=[MARKS, ANY, ANY] + vmem(2) + [ANY, ANY] + vmem(2),
        out_specs=(ANY, ANY, ANY) + tuple(vmem(3)),
        scratch_shapes=[
            pltpu.VMEM((6, 5, EROWS, 128), F32),
            pltpu.VMEM((2, EROWS, 128), F32),
            pltpu.VMEM((5, EROWS, 128), F32),
            pltpu.VMEM((6, BAND, 8, ECOLS), F32),
            band,
            band,
            band,
            band,
            pltpu.VMEM((3, 64, WCOLS), F32),
            pltpu.VMEM((80, COLS), F32),
            pltpu.VMEM((2, ROWS, COLS), jnp.bfloat16),
            pltpu.SemaphoreType.DMA((19,)),
        ],
        compiler_params=PARAMS,
        name="plate",
    )(marks, u, v, d, recv, above_rows, below_rows, above, below)
    from_left = lax.ppermute(resist[:, 128:256], "gy", ahead("gy"))
    tops = exchange(tops, "gx")
    answer = pl.pallas_call(
        solve_kernel,
        out_shape=shaped(GY, 16, CCOLS),
        in_specs=vmem(4),
        out_specs=vmem(1)[0],
        compiler_params=PARAMS,
        name="solve",
    )(resist, from_left, coarse, tops)
    answer = exchange(answer, "gy")
    warmth = pl.pallas_call(
        finish_kernel,
        out_shape=shaped(2, GY * CCOLS),
        in_specs=vmem(2),
        out_specs=vmem(1)[0],
        scratch_shapes=[pltpu.VMEM((2, GY * CCOLS + 128), F32), pltpu.VMEM((7, GY, CCOLS), F32)],
        compiler_params=PARAMS,
        name="finish",
    )(answer, warm)
    return shift, speed, damage, warmth


def solution(mesh):
    tile = P(None, "gx", "gy")
    line = P(("gx", "gy"), None)
    return jax.shard_map(
        per_device,
        mesh=mesh,
        in_specs=(tile, tile, tile, P("gx", "gy"), line, line, line, line),
        out_specs=(tile, tile, tile, line),
        check_vma=False,
    )
```

```python
import jax
import jax.numpy as jnp
from jax import lax
from jax.experimental import pallas as pl
from jax.experimental.pallas import tpu as pltpu
from jax.sharding import PartitionSpec as P

F32 = jnp.float32
ROWS, COLS = 64, 512
CROWS, CCOLS = 32, 256
GX, GY = 8, 16
HALO = 8
HROW = 16
EROWS = ROWS + 2 * HROW
ECOLS = COLS + 128
WCOLS = CCOLS + 128
HEAT_ROWS = CROWS + 8
BAND = EROWS // 8
SUBSTEPS = 8
SEG = 128
TIME_STEP = 0.4
DAMPING = 0.05
EXPANSION = 0.6
LOG2E = 1.4426950408889634
HI = lax.Precision.HIGHEST
CHUNK = 56
CORNER = 16 + 48 + 24 + 24


def lanes(shape):
    return lax.broadcasted_iota(jnp.int32, shape, len(shape) - 1)


def sublanes(shape):
    return lax.broadcasted_iota(jnp.int32, shape, len(shape) - 2)


def turn(value, shift, axis):
    size = value.shape[axis]
    shift %= size
    return value if shift == 0 else pltpu.roll(value, shift, axis)


def mark_rows(weights, first, count):
    parts = [
        jnp.broadcast_to(weights[first // 8 + k : first // 8 + k + 1, :], (8, 128))
        for k in range(count // 8)
    ]
    return jnp.concatenate(parts, axis=0)


def start_all(copies):
    for copy in copies:
        copy.start()


def wait_all(copies):
    for copy in copies:
        copy.wait()


def pack_kernel(
    marks_hbm, u_hbm, v_hbm, d_hbm, warm_hbm, cap_hbm, film_hbm, bath_hbm,
    out, weights,
    marks, u, v, d, warm, cap, film, bath, lines, sem,
):
    pairs = [(marks_hbm, marks)]
    pairs += [(warm_hbm, warm), (cap_hbm, cap), (film_hbm, film), (bath_hbm, bath)]
    for far, near in ((u_hbm, u), (v_hbm, v), (d_hbm, d)):
        for side, at in ((0, 0), (1, COLS - 128)):
            pairs.append((far.at[:, :, pl.ds(at, 128)], near.at[side]))
    copies = [pltpu.make_async_copy(a, b, sem.at[k]) for k, (a, b) in enumerate(pairs)]
    start_all(copies)
    gy = lax.axis_index("gy")
    zero = jnp.zeros((32, 128), F32)
    for g in range(GY):
        out[g, 24:CHUNK, :] = zero
    wait_all(copies[:5])
    for k in range(ROWS // 8):
        weights[k : k + 1, :] = jnp.full((1, 128), marks[k].astype(F32), F32)
    lines[0:2, :] = warm[...]
    lines[2:4, :] = cap[...] + film[...]
    lines[4:6, :] = film[...] * (bath[...] - warm[...])
    lines[6:8, :] = jnp.zeros((2, GY * CCOLS), F32)
    lane = lanes((8, 128))
    for g in range(GY):
        at = g * CCOLS
        out[g, 0:8, :] = lines[:, at : at + 128]
        out[g, 8:16, :] = lines[:, at + 128 : at + 256]
        if g > 0:
            left = lines[:, at - 128 : at]
        else:
            left = jnp.broadcast_to(lines[:, 0:1], (8, 128))
        if g < GY - 1:
            right = lines[:, at + 256 : at + 384]
        else:
            right = jnp.broadcast_to(lines[:, GY * CCOLS - 1 : GY * CCOLS], (8, 128))
        out[g, 16:24, :] = jnp.where(lane < 64, right, left)
    wait_all(copies[5:])

    def edge(side, inner):
        wide = lanes((ROWS, 128))
        weight = mark_rows(weights, 0, ROWS)
        tiles = [u[side, 0], u[side, 1], v[side, 0], v[side, 1]]
        tiles += [1.0 - d[side, f].astype(F32) * (0.125 * weight) for f in range(2)]
        packed = jnp.zeros((ROWS, 128), F32)
        for f, tile in enumerate(tiles + [weight]):
            moved = turn(tile, 8 * f - inner, 1)
            packed = jnp.where((wide >= 8 * f) & (wide < 8 * f + 8), moved, packed)
        return packed[:32] + turn(packed[32:], 64, 1)

    @pl.when(gy < GY - 1)
    def _():
        out[gy + 1, 24:CHUNK, :] = edge(1, 120)

    @pl.when(gy > 0)
    def _():
        out[gy - 1, 24:CHUNK, :] = edge(0, 0)


def rows_kernel(weights, u_hbm, v_hbm, d_hbm, up, down, d, sem):
    copies, levels = [], []
    for m, (message, row0) in enumerate(((up, ROWS - HROW), (down, 0))):
        rows = pl.ds(row0, HROW)
        for k in range(4):
            cols = pl.ds(128 * k, 128)
            for f, far in enumerate((u_hbm, v_hbm)):
                copies.append(
                    pltpu.make_async_copy(
                        far.at[:, rows, cols],
                        message.at[2 * f : 2 * f + 2, k],
                        sem.at[8 * m + 2 * k + f],
                    )
                )
        levels.append(pltpu.make_async_copy(d_hbm.at[:, rows, :], d.at[m], sem.at[16 + m]))
    start_all(levels + copies)
    wait_all(levels)
    for m, (message, row0) in enumerate(((up, ROWS - HROW), (down, 0))):
        weight = 0.125 * mark_rows(weights, row0, HROW)
        for f in range(2):
            for k in range(4):
                level = d[m, f, :, pl.ds(128 * k, 128)].astype(F32)
                message[4 + f, k] = 1.0 - level * weight
    wait_all(copies)


def join_sides(f, left, left_at, right, right_at):
    lane = lanes(left.shape)
    from_right = turn(right, -(right_at + 8 * f), 1)
    from_left = turn(left, 120 - left_at - 8 * f, 1)
    return jnp.where(lane < 8, from_right, jnp.where(lane >= 120, from_left, 0.0))


def sides(recv):
    gy = lax.axis_index("gy")
    left = recv[jnp.maximum(gy - 1, 0), 24:CHUNK, :]
    right = recv[jnp.minimum(gy + 1, GY - 1), 24:CHUNK, :]
    return left, right


def rim_kernel(weights, recv, up, down):
    left, right = sides(recv)
    lane = lanes((HROW, 128))
    for out, row0, coarse0, thin0 in ((up, ROWS - HROW, 16, 24), (down, 0, 0, 0)):
        if row0 == 0:
            near, off = left[0:16], turn(right[0:16], 64, 1)
        else:
            near, off = turn(left[16:32], 64, 1), right[16:32]
        corner = jnp.where(lane < 56, near, off)
        out[0:16, :] = jnp.where(
            (lane >= 56) & (lane < 64), mark_rows(weights, row0, HROW), corner
        )
        for k in range(3):
            for r in range(0, 16, 2):
                g = (coarse0 + r) // 2
                out[16 + 16 * k + r : 18 + 16 * k + r, :] = recv[g, 8 * k : 8 * k + 2, :]
            for r in range(0, 8, 2):
                g = (thin0 + r) // 2
                for a, base in ((1, 64), (2, 88)):
                    out[base + 8 * k + r : base + 8 * k + r + 2, :] = recv[
                        g, 8 * k + 2 * a : 8 * k + 2 * a + 2, :
                    ]


def strip_of(t):
    return pl.ds(t, 8, stride=BAND)


def prep_kernel(
    weights, u, v, d, recv, above_rows, below_rows,
    state, side, coarse, table,
    field, sem,
):
    gx = lax.axis_index("gx")
    gy = lax.axis_index("gy")
    top = pl.ds(0, HROW)
    mid = pl.ds(HROW, ROWS)
    low = pl.ds(HROW + ROWS, HROW)
    copies = [
        pltpu.make_async_copy(above_rows, field.at[:, :, top], sem.at[0]),
        pltpu.make_async_copy(below_rows, field.at[:, :, low], sem.at[1]),
    ]
    for k in range(4):
        cols = pl.ds(128 * k, 128)
        for f, source in enumerate((u, v)):
            here = field.at[2 * f : 2 * f + 2, k, mid]
            copies.append(pltpu.make_async_copy(source.at[:, :, cols], here, sem.at[2 + 2 * k + f]))
    start_all(copies)
    left, right = sides(recv)
    for k in range(3):
        cols = pl.ds(128 * k, 128)
        for g in range(GY):
            for a in range(3):
                coarse[a, 2 * g : 2 * g + 2, cols] = recv[g, 8 * k + 2 * a : 8 * k + 2 * a + 2, :]
    p = sublanes((256, 128))
    q = lanes((256, 128))
    place = (p % SEG).astype(F32)
    even = (2 * (q % 64)).astype(F32)
    spread = jnp.exp(jnp.abs(place - even) * (-4.0 / SEG)) + jnp.exp(
        jnp.abs(place - even - 1.0) * (-4.0 / SEG)
    )
    table[...] = jnp.where(p // SEG == q // 64, spread * (0.5 * 2.0 / SEG), 0.0)
    for f in range(7):
        for half in (0, 32):
            side[f, pl.ds(half, 32), :] = join_sides(
                f, left, half * 2, right, half * 2
            )
    weight = 0.125 * mark_rows(weights, 0, ROWS)
    for f in range(2):
        for k in range(4):
            level = d[f, :, pl.ds(128 * k, 128)].astype(F32)
            field[4 + f, k, mid, :] = 1.0 - level * weight
    wait_all(copies)
    lane = lanes((8, 128))
    first = gx * ROWS - HROW + BAND * sublanes((8, 128))
    for t in range(BAND):
        row = first + t
        inner_row = (row >= 1) & (row < GX * ROWS)
        for k in range(4):
            cols = pl.ds(128 * k, 128)
            for f in range(4):
                state[f, t, :, cols] = field[f, k, strip_of(t), :]
            state[4, t, :, cols] = jnp.where(inner_row, field[4, k, strip_of(t), :], 0.0)
            spring = field[5, k, strip_of(t), :]
            if k == 0:
                spring = jnp.where(gy * COLS + lane >= 1, spring, 0.0)
            state[5, t, :, cols] = spring


def plate_kernel(
    weights, state_in, side, coarse_in, table, above, below,
    shift_out, speed_out, damage_out, resist_out, coarse_out, edge_out,
    field, cw, temp, state, rate, warmth, tx, ty, coarse, gap, worn, sem,
):
    gx = lax.axis_index("gx")
    gy = lax.axis_index("gy")
    top = pl.ds(0, HROW)
    mid = pl.ds(HROW, ROWS)
    low = pl.ds(HROW + ROWS, HROW)
    main = pl.ds(0, COLS)
    fetch = pltpu.make_async_copy(
        state_in.at[:, :, :, main], state.at[:, :, :, main], sem.at[9]
    )
    fetch.start()
    results = []
    for k in range(4):
        cols = pl.ds(128 * k, 128)
        for f, target in enumerate((shift_out, speed_out)):
            here = field.at[2 * f : 2 * f + 2, k, mid]
            results.append(
                pltpu.make_async_copy(here, target.at[:, :, cols], sem.at[2 * k + f])
            )
    results.append(pltpu.make_async_copy(worn, damage_out, sem.at[8]))

    coarse[:, 16:48, :] = coarse_in[...]
    for k in range(3):
        cols = pl.ds(128 * k, 128)
        coarse[0, 0:16, cols] = above[16 + 16 * k : 32 + 16 * k, :]
        coarse[0, 48:64, cols] = below[16 + 16 * k : 32 + 16 * k, :]
        for a, base in ((1, 64), (2, 88)):
            coarse[a, 8:16, cols] = above[base + 8 * k : base + 8 * k + 8, :]
            coarse[a, 48:56, cols] = below[base + 8 * k : base + 8 * k + 8, :]

    @pl.when(gx == 0)
    def _():
        coarse[0, 0:16, :] = jnp.broadcast_to(coarse[0, 16:17, :], (16, WCOLS))
        coarse[1, 8:16, :] = jnp.ones((8, WCOLS), F32)

    @pl.when(gx == GX - 1)
    def _():
        coarse[0, 48:64, :] = jnp.broadcast_to(coarse[0, 47:48, :], (16, WCOLS))
        coarse[1, 48:56, :] = jnp.ones((8, WCOLS), F32)

    coarse_out[...] = coarse[:, 12 : 12 + HEAT_ROWS, :]

    p = sublanes((128, 128))
    q = lanes((128, 128))
    middle = 32 + q // 2
    beside = middle + 2 * (q % 2) - 1
    widen = jnp.where(p == middle, 0.75, 0.0) + jnp.where(p == beside, 0.25, 0.0)
    i = sublanes((EROWS, 64))
    c = lanes((EROWS, 64))
    middle = 8 + i // 2
    beside = middle + 2 * (i % 2) - 1
    raise_ = jnp.where(c == middle, 0.75, 0.0) + jnp.where(c == beside, 0.25, 0.0)
    warm = coarse[0]

    def columns(k):
        window = turn(warm, 32 - 64 * k, 1)[:, 0:128]
        return jnp.dot(window, widen, precision=HI, preferred_element_type=F32)

    lane64 = lanes((64, 128))
    tiles = [columns(k) for k in range(4)]
    tiles.append(jnp.where(lane64 < 64, columns(4), columns(-1)))
    for k in range(5):
        temp[k] = jnp.dot(raise_, tiles[k], precision=HI, preferred_element_type=F32)

    factor = -4.0 * LOG2E
    for rows, source in ((top, above), (low, below)):
        tile = source[0:16, :]
        for f in range(6):
            field[f, 4, rows, :] = join_sides(f, tile, 0, tile, 64)
        cw[1, rows, :] = factor * join_sides(6, tile, 0, tile, 64)
        cw[0, rows, :] = jnp.broadcast_to(factor * tile[:, 60:61], (HROW, 128))
    for f in range(6):
        field[f, 4, mid, :] = side[f]
    cw[1, mid, :] = factor * side[6]
    cw[0, mid, :] = factor * mark_rows(weights, 0, ROWS)

    lane = lanes((8, 128))
    first = gx * ROWS - HROW + BAND * sublanes((8, 128))
    rest = pl.ds(COLS, 128)
    col = gy * COLS + jnp.where(lane < 64, lane + COLS, lane - 128)
    inner_col = (col >= 1) & (col < GY * COLS)
    for t in range(BAND):
        row = first + t
        inner_row = (row >= 1) & (row < GX * ROWS)
        own_rate = cw[0, strip_of(t), :]
        for k in range(4):
            rate[t, :, pl.ds(128 * k, 128)] = own_rate
        rate[t, :, rest] = cw[1, strip_of(t), :]
        for k in range(5):
            warmth[t, :, pl.ds(128 * k, 128)] = (0.5 * EXPANSION) * temp[k, strip_of(t), :]
        for f in range(4):
            state[f, t, :, rest] = field[f, 4, strip_of(t), :]
        state[4, t, :, rest] = jnp.where(inner_row, field[4, 4, strip_of(t), :], 0.0)
        state[5, t, :, rest] = jnp.where(inner_col, field[5, 4, strip_of(t), :], 0.0)
    before = turn(warmth[BAND - 1], 1, 0)
    for t in range(BAND):
        own = warmth[t]
        tx[t] = own + before
        ty[t] = own + turn(own, 1, 1)
        before = own
    fetch.wait()

    keep = 1.0 - TIME_STEP * DAMPING

    def edge_x(t, a0, a1, o0, o1):
        open_x = a0 - o0 - tx[t]
        stretch = jnp.maximum(open_x, 0.0)
        spring = jnp.minimum(state[4, t], jnp.exp2(rate[t] * (stretch * stretch)))
        state[4, t] = spring
        return spring * open_x, spring * (a1 - o1)

    def substep(_, carry):
        a0, a1 = state[0, BAND - 1], state[1, BAND - 1]
        first_nx, first_ax = edge_x(0, state[0, 0], state[1, 0], turn(a0, 1, 0), turn(a1, 1, 0))
        next_nx, next_ax = turn(first_nx, -1, 0), turn(first_ax, -1, 0)
        for t in reversed(range(BAND)):
            open_y = a1 - turn(a1, 1, 1) - ty[t]
            stretch = jnp.maximum(open_y, 0.0)
            spring = jnp.minimum(state[5, t], jnp.exp2(rate[t] * (stretch * stretch)))
            state[5, t] = spring
            ny = spring * open_y
            ay = spring * (a0 - turn(a0, 1, 1))
            if t > 0:
                o0, o1 = state[0, t - 1], state[1, t - 1]
                nx, ax = edge_x(t, a0, a1, o0, o1)
            else:
                o0, o1 = a0, a1
                nx, ax = first_nx, first_ax
            force0 = (next_nx - nx) + (turn(ay, -1, 1) - ay)
            force1 = (next_ax - ax) + (turn(ny, -1, 1) - ny)
            next_nx, next_ax = nx, ax
            b0 = keep * state[2, t] + TIME_STEP * force0
            b1 = keep * state[3, t] + TIME_STEP * force1
            state[2, t] = b0
            state[3, t] = b1
            state[0, t] = a0 + TIME_STEP * b0
            state[1, t] = a1 + TIME_STEP * b1
            a0, a1 = o0, o1
        return carry

    lax.fori_loop(0, SUBSTEPS, substep, 0)
    for f in range(6):
        for t in range(BAND):
            for k in range(4):
                field[f, k, pl.ds(t, 8, stride=BAND), :] = state[f, t, :, pl.ds(128 * k, 128)]
        if f == 3:
            start_all(results[:-1])
    for b in range(10):
        rows = pl.ds(8 + 8 * b, 8)
        row = gx * ROWS - 8 + 8 * b + sublanes((8, 128))
        for k in range(4):
            cols = pl.ds(128 * k, 128)
            dx = jnp.where(row >= 1, 1.0 - field[4, k, rows, :], 0.0)
            dy = 1.0 - field[5, k, rows, :]
            if k == 0:
                dy = jnp.where(gy * COLS + lane >= 1, dy, 0.0)
            gap[pl.ds(8 * b, 8), cols] = dx + dy
            if 1 <= b < 9:
                worn[0, pl.ds(8 * b - 8, 8), cols] = dx.astype(jnp.bfloat16)
                worn[1, pl.ds(8 * b - 8, 8), cols] = dy.astype(jnp.bfloat16)
    start_all(results[-1:])
    a = sublanes((HEAT_ROWS, 2 * HEAT_ROWS))
    c = lanes((HEAT_ROWS, 2 * HEAT_ROWS))
    pool = jnp.where(c // 2 == a, 1.0, 0.0)
    for k in range(2):
        pair = jnp.dot(pool, gap[:, pl.ds(256 * k, 256)], precision=HI, preferred_element_type=F32)
        resist_out[:, pl.ds(128 * k, 128)] = jnp.dot(
            pair, table[...], precision=HI, preferred_element_type=F32
        )
    edge_out[...] = resist_out[:, 128:256]
    wait_all(results)


def border_kernel(resist, coarse, out):
    gx = lax.axis_index("gx")
    conduct = (1.0 + 0.5 * coarse[0, :, 0:CCOLS]) / (1.0 + resist[...])
    shape = (HEAT_ROWS, CCOLS)
    row = gx * CROWS - 4 + sublanes(shape)
    down = jnp.where((row >= 1) & (row < GX * CROWS), 0.5 * (conduct + turn(conduct, 1, 0)), 0.0)
    side = jnp.where(lanes(shape) >= 1, 0.5 * (conduct + turn(conduct, 1, 1)), 0.0)
    offsum = (down + turn(down, -1, 0) + side + turn(side, -1, 1))[4 : 4 + CROWS]
    capacity = coarse[1, 4 : 4 + CROWS, 0:CCOLS]
    top = jnp.max(offsum / (capacity + offsum), axis=(0, 1), keepdims=True)
    a = sublanes((8, CCOLS))
    c = lanes((8, CCOLS))
    border = jnp.where(sublanes((8, 128)) >= 6, top, 0.0)
    for k, value in enumerate((offsum, capacity, conduct[4 : 4 + CROWS])):
        pick = jnp.where(
            ((a == 2 * k) & (c == 0)) | ((a == 2 * k + 1) & (c == CCOLS - 1)), 1.0, 0.0
        )
        border += lax.dot_general(
            pick,
            jnp.concatenate([value] * 4, axis=0),
            (((1,), (1,)), ((), ())),
            precision=HI,
            preferred_element_type=F32,
        )
    for g in range(GX):
        out[g] = border


def conductances(resist, from_left, coarse):
    gx = lax.axis_index("gx")
    gy = lax.axis_index("gy")
    shape = (HEAT_ROWS, WCOLS)
    lane = lanes((HEAT_ROWS, 128))
    rim = jnp.where(lane < 64, 0.0, from_left[...])
    wide = jnp.concatenate([resist[...], rim], axis=1)
    warm = coarse[0]
    conduct = (1.0 + 0.5 * warm) / (1.0 + wide)
    row = gx * CROWS - 4 + sublanes(shape)
    lane = lanes(shape)
    col = gy * CCOLS + jnp.where(lane < CCOLS + 64, lane, lane - WCOLS)
    down = jnp.where(
        (row >= 1) & (row < GX * CROWS), 0.5 * (conduct + turn(conduct, 1, 0)), 0.0
    )
    side = jnp.where(
        (col >= 1) & (col < GY * CCOLS), 0.5 * (conduct + turn(conduct, 1, 1)), 0.0
    )
    up = turn(down, -1, 0)
    far = turn(side, -1, 1)
    offsum = down + up + side + far
    return warm, down, up, side, far, offsum, coarse[1] + offsum


def solve_kernel(resist, from_left, coarse, tops, out):
    warm, down, up, side, far, _, diagonal = conductances(resist, from_left, coarse)
    inverse = 1.0 / diagonal

    def spread(x):
        return (
            down * turn(x, 1, 0) + up * turn(x, -1, 0) + side * turn(x, 1, 1) + far * turn(x, -1, 1)
        ) * inverse

    start = coarse[2] + (
        down * (turn(warm, 1, 0) - warm)
        + up * (turn(warm, -1, 0) - warm)
        + side * (turn(warm, 1, 1) - warm)
        + far * (turn(warm, -1, 1) - warm)
    )
    z = start * inverse
    y = z + spread(z)
    y2 = turn(spread(spread(y)), 4, 1)
    y = turn(y, 4, 1)
    group = lanes((8, 128)) // 32
    strip = []
    for h in range(2):
        tile = tops[4 * h]
        for k in range(1, 4):
            tile = jnp.where(group == k, tops[4 * h + k], tile)
        strip.append(tile)
    last_y, last_y2 = y[:, CCOLS:], turn(y2[:, CCOLS:], 64, 1)
    tail = jnp.where(lanes(last_y.shape) < 64, last_y, last_y2)
    for g in range(GY):
        rows = slice(4 + 2 * g, 6 + 2 * g)
        for h in range(2):
            cols = slice(128 * h, 128 * h + 128)
            out[g, 2 * h : 2 * h + 2, :] = y[rows, cols]
            out[g, 4 + 2 * h : 6 + 2 * h, :] = y2[rows, cols]
            out[g, 8 + 8 * h : 16 + 8 * h, :] = strip[h]
            out[g, 15 + 8 * h : 16 + 8 * h, :] = tail[4 + 2 * g + h : 5 + 2 * g + h]


def finish_kernel(recv, warm, out, wide, border):
    for g in range(GY):
        for k in range(7):
            for h in range(2):
                border[k, g : g + 1, pl.ds(128 * h, 128)] = recv[g, 8 + 8 * h + k : 9 + 8 * h + k, :]
    across = 0.5 * (turn(border[5], 1, 0) + border[4])
    across = jnp.where(sublanes((GY, CCOLS)) >= 1, across, 0.0)
    top = border[6]
    for k, face in ((0, across), (1, turn(across, -1, 0))):
        offsum = border[k] + face
        top = jnp.maximum(top, offsum / (border[2 + k] + offsum))
    top = jnp.max(top, axis=(0, 1), keepdims=True)
    square = top * top
    gain = 8.0 / (8.0 - 8.0 * square + square * square)
    near = gain * (1.0 - square)
    for g in range(GY):
        for h in range(2):
            wide[:, pl.ds(CCOLS * g + 128 * h, 128)] = (
                near * recv[g, 2 * h : 2 * h + 2, :] + gain * recv[g, 4 + 2 * h : 6 + 2 * h, :]
            )
    for h in range(2):
        tail = recv[GY - 1, 15 + 8 * h : 16 + 8 * h, :]
        wide[h : h + 1, pl.ds(CCOLS * GY, 128)] = near * tail + gain * turn(tail, 64, 1)
    out[...] = warm[...] + turn(wide[...], -4, 1)[:, : GY * CCOLS]


def vmem(count):
    return [pl.BlockSpec(memory_space=pltpu.VMEM)] * count


ANY = pl.BlockSpec(memory_space=pl.ANY)
FAR = pl.BlockSpec(memory_space=pltpu.MemorySpace.HBM)
PARAMS = pltpu.CompilerParams(vmem_limit_bytes=32 * 1024 * 1024)


def shaped(*shape, dtype=F32):
    return jax.ShapeDtypeStruct(shape, dtype)


def ahead(axis):
    count = lax.axis_size(axis)
    return [(i, (i + 1) % count) for i in range(count)]


def neighbours(value_up, value_down, axis):
    back = [(j, i) for i, j in ahead(axis)]
    return lax.ppermute(value_up, axis, ahead(axis)), lax.ppermute(value_down, axis, back)


def exchange(value, axis):
    return lax.all_to_all(value, axis, split_axis=0, concat_axis=0, tiled=True)


def per_device(u, v, d, marks, warm, cap, film, bath):
    far = [
        pltpu.with_memory_space_constraint(x, pltpu.MemorySpace.HBM)
        for x in (marks.reshape(ROWS // 8), u, v, d, warm, cap, film, bath)
    ]
    side = pltpu.VMEM((2, 2, ROWS, 128), F32)
    line = pltpu.VMEM((2, GY * CCOLS), F32)
    packed, weights = pl.pallas_call(
        pack_kernel,
        out_shape=(shaped(GY, CHUNK, 128), shaped(8, 128)),
        in_specs=[FAR] * 8,
        out_specs=tuple(vmem(2)),
        scratch_shapes=[pltpu.SMEM((ROWS // 8,), jnp.int32)]
        + [side, side, pltpu.VMEM((2, 2, ROWS, 128), jnp.int32)]
        + [line] * 4
        + [pltpu.VMEM((8, GY * CCOLS), F32), pltpu.SemaphoreType.DMA((11,))],
        compiler_params=PARAMS,
        name="pack",
    )(*far)
    recv = exchange(packed, "gy")
    up_rows, down_rows = pl.pallas_call(
        rows_kernel,
        out_shape=(shaped(6, 4, HROW, 128), shaped(6, 4, HROW, 128)),
        in_specs=vmem(1) + [FAR] * 3,
        out_specs=tuple(vmem(2)),
        scratch_shapes=[
            pltpu.VMEM((2, 2, HROW, COLS), jnp.int32),
            pltpu.SemaphoreType.DMA((18,)),
        ],
        compiler_params=PARAMS,
        name="rows",
    )(weights, *far[1:4])
    above_rows, below_rows = neighbours(up_rows, down_rows, "gx")
    up, down = pl.pallas_call(
        rim_kernel,
        out_shape=(shaped(CORNER, 128), shaped(CORNER, 128)),
        in_specs=vmem(2),
        out_specs=tuple(vmem(2)),
        compiler_params=PARAMS,
        name="rim",
    )(weights, recv)
    above, below = neighbours(up, down, "gx")
    state, side, coarse, table = pl.pallas_call(
        prep_kernel,
        out_shape=(
            shaped(6, BAND, 8, ECOLS),
            shaped(7, ROWS, 128),
            shaped(3, CROWS, WCOLS),
            shaped(256, 128),
        ),
        in_specs=vmem(1) + [ANY, ANY] + vmem(2) + [ANY, ANY],
        out_specs=tuple(vmem(4)),
        scratch_shapes=[
            pltpu.VMEM((6, 4, EROWS, 128), F32),
            pltpu.SemaphoreType.DMA((10,)),
        ],
        compiler_params=PARAMS,
        name="prep",
    )(weights, u, v, d, recv, above_rows, below_rows)
    band = pltpu.VMEM((BAND, 8, ECOLS), F32)
    shift, speed, damage, resist, coarse, edge = pl.pallas_call(
        plate_kernel,
        out_shape=(
            shaped(2, ROWS, COLS),
            shaped(2, ROWS, COLS),
            shaped(2, ROWS, COLS, dtype=jnp.bfloat16),
            shaped(HEAT_ROWS, CCOLS),
            shaped(3, HEAT_ROWS, WCOLS),
            shaped(HEAT_ROWS, 128),
        ),
        in_specs=vmem(1) + [ANY] + vmem(5),
        out_specs=(ANY, ANY, ANY) + tuple(vmem(3)),
        scratch_shapes=[
            pltpu.VMEM((6, 5, EROWS, 128), F32),
            pltpu.VMEM((2, EROWS, 128), F32),
            pltpu.VMEM((5, EROWS, 128), F32),
            pltpu.VMEM((6, BAND, 8, ECOLS), F32),
            band,
            band,
            band,
            band,
            pltpu.VMEM((3, 64, WCOLS), F32),
            pltpu.VMEM((80, COLS), F32),
            pltpu.VMEM((2, ROWS, COLS), jnp.bfloat16),
            pltpu.SemaphoreType.DMA((10,)),
        ],
        compiler_params=PARAMS,
        name="plate",
    )(weights, state, side, coarse, table, above, below)
    from_left = lax.ppermute(edge, "gy", ahead("gy"))
    tops = pl.pallas_call(
        border_kernel,
        out_shape=shaped(GX, 8, 128),
        in_specs=vmem(2),
        out_specs=vmem(1)[0],
        compiler_params=PARAMS,
        name="border",
    )(resist, coarse)
    tops = exchange(tops, "gx")
    answer = pl.pallas_call(
        solve_kernel,
        out_shape=shaped(GY, 24, 128),
        in_specs=vmem(4),
        out_specs=vmem(1)[0],
        compiler_params=PARAMS,
        name="solve",
    )(resist, from_left, coarse, tops)
    answer = exchange(answer, "gy")
    warmth = pl.pallas_call(
        finish_kernel,
        out_shape=shaped(2, GY * CCOLS),
        in_specs=vmem(2),
        out_specs=vmem(1)[0],
        scratch_shapes=[pltpu.VMEM((2, GY * CCOLS + 128), F32), pltpu.VMEM((7, GY, CCOLS), F32)],
        compiler_params=PARAMS,
        name="finish",
    )(answer, warm)
    return shift, speed, damage, warmth


def solution(mesh):
    tile = P(None, "gx", "gy")
    line = P(("gx", "gy"), None)
    return jax.shard_map(
        per_device,
        mesh=mesh,
        in_specs=(tile, tile, tile, P("gx", "gy"), line, line, line, line),
        out_specs=(tile, tile, tile, line),
        check_vma=False,
    )
```

```python
import jax
import jax.numpy as jnp
from jax import lax
from jax.experimental import pallas as pl
from jax.experimental.pallas import tpu as pltpu
from jax.sharding import PartitionSpec as P

F32 = jnp.float32
ROWS, COLS = 64, 512
CROWS, CCOLS = 32, 256
GX, GY = 8, 16
HALO = 8
HROW = 16
EROWS = ROWS + 2 * HROW
ECOLS = COLS + 128
WCOLS = CCOLS + 128
HEAT_ROWS = CROWS + 8
BAND = EROWS // 8
SUBSTEPS = 8
SEG = 128
TIME_STEP = 0.4
DAMPING = 0.05
EXPANSION = 0.6
LOG2E = 1.4426950408889634
HI = lax.Precision.HIGHEST
CHUNK = 56
CORNER = 16 + 48 + 24 + 24


def lanes(shape):
    return lax.broadcasted_iota(jnp.int32, shape, len(shape) - 1)


def sublanes(shape):
    return lax.broadcasted_iota(jnp.int32, shape, len(shape) - 2)


def turn(value, shift, axis):
    size = value.shape[axis]
    shift %= size
    return value if shift == 0 else pltpu.roll(value, shift, axis)


def mark_rows(weights, first, count):
    parts = [
        jnp.broadcast_to(weights[first // 8 + k : first // 8 + k + 1, :], (8, 128))
        for k in range(count // 8)
    ]
    return jnp.concatenate(parts, axis=0)


def start_all(copies):
    for copy in copies:
        copy.start()


def wait_all(copies):
    for copy in copies:
        copy.wait()


def pack_kernel(
    marks_hbm, u_hbm, v_hbm, d_hbm, warm_hbm, cap_hbm, film_hbm, bath_hbm,
    out, weights,
    marks, u, v, d, warm, cap, film, bath, lines, sem,
):
    pairs = [(marks_hbm, marks)]
    pairs += [(warm_hbm, warm), (cap_hbm, cap), (film_hbm, film), (bath_hbm, bath)]
    for far, near in ((u_hbm, u), (v_hbm, v), (d_hbm, d)):
        for side, at in ((0, 0), (1, COLS - 128)):
            pairs.append((far.at[:, :, pl.ds(at, 128)], near.at[side]))
    copies = [pltpu.make_async_copy(a, b, sem.at[k]) for k, (a, b) in enumerate(pairs)]
    start_all(copies)
    gy = lax.axis_index("gy")
    zero = jnp.zeros((32, 128), F32)
    for g in range(GY):
        out[g, 24:CHUNK, :] = zero
    wait_all(copies[:5])
    for k in range(ROWS // 8):
        weights[k : k + 1, :] = jnp.full((1, 128), marks[k].astype(F32), F32)
    lines[0:2, :] = warm[...]
    lines[2:4, :] = cap[...] + film[...]
    lines[4:6, :] = film[...] * (bath[...] - warm[...])
    lines[6:8, :] = jnp.zeros((2, GY * CCOLS), F32)
    lane = lanes((8, 128))
    for g in range(GY):
        at = g * CCOLS
        out[g, 0:8, :] = lines[:, at : at + 128]
        out[g, 8:16, :] = lines[:, at + 128 : at + 256]
        if g > 0:
            left = lines[:, at - 128 : at]
        else:
            left = jnp.broadcast_to(lines[:, 0:1], (8, 128))
        if g < GY - 1:
            right = lines[:, at + 256 : at + 384]
        else:
            right = jnp.broadcast_to(lines[:, GY * CCOLS - 1 : GY * CCOLS], (8, 128))
        out[g, 16:24, :] = jnp.where(lane < 64, right, left)
    wait_all(copies[5:])

    def edge(side, inner):
        wide = lanes((ROWS, 128))
        weight = mark_rows(weights, 0, ROWS)
        tiles = [u[side, 0], u[side, 1], v[side, 0], v[side, 1]]
        tiles += [1.0 - d[side, f].astype(F32) * (0.125 * weight) for f in range(2)]
        packed = jnp.zeros((ROWS, 128), F32)
        for f, tile in enumerate(tiles + [weight]):
            moved = turn(tile, 8 * f - inner, 1)
            packed = jnp.where((wide >= 8 * f) & (wide < 8 * f + 8), moved, packed)
        return packed[:32] + turn(packed[32:], 64, 1)

    @pl.when(gy < GY - 1)
    def _():
        out[gy + 1, 24:CHUNK, :] = edge(1, 120)

    @pl.when(gy > 0)
    def _():
        out[gy - 1, 24:CHUNK, :] = edge(0, 0)


def rows_kernel(weights, u_hbm, v_hbm, d_hbm, up, down, d, sem):
    copies, levels = [], []
    for m, (message, row0) in enumerate(((up, ROWS - HROW), (down, 0))):
        rows = pl.ds(row0, HROW)
        for k in range(4):
            cols = pl.ds(128 * k, 128)
            for f, far in enumerate((u_hbm, v_hbm)):
                copies.append(
                    pltpu.make_async_copy(
                        far.at[:, rows, cols],
                        message.at[2 * f : 2 * f + 2, k],
                        sem.at[8 * m + 2 * k + f],
                    )
                )
        levels.append(pltpu.make_async_copy(d_hbm.at[:, rows, :], d.at[m], sem.at[16 + m]))
    start_all(levels + copies)
    wait_all(levels)
    for m, (message, row0) in enumerate(((up, ROWS - HROW), (down, 0))):
        weight = 0.125 * mark_rows(weights, row0, HROW)
        for f in range(2):
            for k in range(4):
                level = d[m, f, :, pl.ds(128 * k, 128)].astype(F32)
                message[4 + f, k] = 1.0 - level * weight
    wait_all(copies)


def join_sides(f, left, left_at, right, right_at):
    lane = lanes(left.shape)
    from_right = turn(right, -(right_at + 8 * f), 1)
    from_left = turn(left, 120 - left_at - 8 * f, 1)
    return jnp.where(lane < 8, from_right, jnp.where(lane >= 120, from_left, 0.0))


def sides(recv):
    gy = lax.axis_index("gy")
    left = recv[jnp.maximum(gy - 1, 0), 24:CHUNK, :]
    right = recv[jnp.minimum(gy + 1, GY - 1), 24:CHUNK, :]
    return left, right


def rim_kernel(weights, recv, up, down):
    left, right = sides(recv)
    lane = lanes((HROW, 128))
    for out, row0, coarse0, thin0 in ((up, ROWS - HROW, 16, 24), (down, 0, 0, 0)):
        if row0 == 0:
            near, off = left[0:16], turn(right[0:16], 64, 1)
        else:
            near, off = turn(left[16:32], 64, 1), right[16:32]
        corner = jnp.where(lane < 56, near, off)
        out[0:16, :] = jnp.where(
            (lane >= 56) & (lane < 64), mark_rows(weights, row0, HROW), corner
        )
        for k in range(3):
            for r in range(0, 16, 2):
                g = (coarse0 + r) // 2
                out[16 + 16 * k + r : 18 + 16 * k + r, :] = recv[g, 8 * k : 8 * k + 2, :]
            for r in range(0, 8, 2):
                g = (thin0 + r) // 2
                for a, base in ((1, 64), (2, 88)):
                    out[base + 8 * k + r : base + 8 * k + r + 2, :] = recv[
                        g, 8 * k + 2 * a : 8 * k + 2 * a + 2, :
                    ]


def strip_of(t):
    return pl.ds(t, 8, stride=BAND)


def prep_kernel(
    weights, u, v, d, recv, above_rows, below_rows,
    state, side, coarse, table,
    field, sem,
):
    gx = lax.axis_index("gx")
    gy = lax.axis_index("gy")
    top = pl.ds(0, HROW)
    mid = pl.ds(HROW, ROWS)
    low = pl.ds(HROW + ROWS, HROW)
    copies = [
        pltpu.make_async_copy(above_rows, field.at[:, :, top], sem.at[0]),
        pltpu.make_async_copy(below_rows, field.at[:, :, low], sem.at[1]),
    ]
    for k in range(4):
        cols = pl.ds(128 * k, 128)
        for f, source in enumerate((u, v)):
            here = field.at[2 * f : 2 * f + 2, k, mid]
            copies.append(pltpu.make_async_copy(source.at[:, :, cols], here, sem.at[2 + 2 * k + f]))
    start_all(copies)
    left, right = sides(recv)
    for k in range(3):
        cols = pl.ds(128 * k, 128)
        for g in range(GY):
            for a in range(3):
                coarse[a, 2 * g : 2 * g + 2, cols] = recv[g, 8 * k + 2 * a : 8 * k + 2 * a + 2, :]
    p = sublanes((256, 128))
    q = lanes((256, 128))
    place = (p % SEG).astype(F32)
    even = (2 * (q % 64)).astype(F32)
    spread = jnp.exp(jnp.abs(place - even) * (-4.0 / SEG)) + jnp.exp(
        jnp.abs(place - even - 1.0) * (-4.0 / SEG)
    )
    table[...] = jnp.where(p // SEG == q // 64, spread * (0.5 * 2.0 / SEG), 0.0)
    for f in range(7):
        for half in (0, 32):
            side[f, pl.ds(half, 32), :] = join_sides(
                f, left, half * 2, right, half * 2
            )
    weight = 0.125 * mark_rows(weights, 0, ROWS)
    for f in range(2):
        for k in range(4):
            level = d[f, :, pl.ds(128 * k, 128)].astype(F32)
            field[4 + f, k, mid, :] = 1.0 - level * weight
    wait_all(copies)
    lane = lanes((8, 128))
    first = gx * ROWS - HROW + BAND * sublanes((8, 128))
    for t in range(BAND):
        row = first + t
        inner_row = (row >= 1) & (row < GX * ROWS)
        for k in range(4):
            cols = pl.ds(128 * k, 128)
            for f in range(4):
                state[f, t, :, cols] = field[f, k, strip_of(t), :]
            state[4, t, :, cols] = jnp.where(inner_row, field[4, k, strip_of(t), :], 0.0)
            spring = field[5, k, strip_of(t), :]
            if k == 0:
                spring = jnp.where(gy * COLS + lane >= 1, spring, 0.0)
            state[5, t, :, cols] = spring


def plate_kernel(
    weights, state_in, side, coarse_in, table, above, below,
    shift_out, speed_out, damage_out, resist_out, coarse_out, edge_out, tops_out,
    field, cw, temp, state, rate, warmth, tx, ty, coarse, gap, worn, border_tiles, sem,
):
    gx = lax.axis_index("gx")
    gy = lax.axis_index("gy")
    top = pl.ds(0, HROW)
    mid = pl.ds(HROW, ROWS)
    low = pl.ds(HROW + ROWS, HROW)
    main = pl.ds(0, COLS)
    fetch = pltpu.make_async_copy(
        state_in.at[:, :, :, main], state.at[:, :, :, main], sem.at[9]
    )
    fetch.start()
    results = []
    for k in range(4):
        cols = pl.ds(128 * k, 128)
        for f, target in enumerate((shift_out, speed_out)):
            here = field.at[2 * f : 2 * f + 2, k, mid]
            results.append(
                pltpu.make_async_copy(here, target.at[:, :, cols], sem.at[2 * k + f])
            )
    results.append(pltpu.make_async_copy(worn, damage_out, sem.at[8]))

    coarse[:, 16:48, :] = coarse_in[...]
    for k in range(3):
        cols = pl.ds(128 * k, 128)
        coarse[0, 0:16, cols] = above[16 + 16 * k : 32 + 16 * k, :]
        coarse[0, 48:64, cols] = below[16 + 16 * k : 32 + 16 * k, :]
        for a, base in ((1, 64), (2, 88)):
            coarse[a, 8:16, cols] = above[base + 8 * k : base + 8 * k + 8, :]
            coarse[a, 48:56, cols] = below[base + 8 * k : base + 8 * k + 8, :]

    @pl.when(gx == 0)
    def _():
        coarse[0, 0:16, :] = jnp.broadcast_to(coarse[0, 16:17, :], (16, WCOLS))
        coarse[1, 8:16, :] = jnp.ones((8, WCOLS), F32)

    @pl.when(gx == GX - 1)
    def _():
        coarse[0, 48:64, :] = jnp.broadcast_to(coarse[0, 47:48, :], (16, WCOLS))
        coarse[1, 48:56, :] = jnp.ones((8, WCOLS), F32)

    coarse_out[...] = coarse[:, 12 : 12 + HEAT_ROWS, :]

    p = sublanes((128, 128))
    q = lanes((128, 128))
    middle = 32 + q // 2
    beside = middle + 2 * (q % 2) - 1
    widen = jnp.where(p == middle, 0.75, 0.0) + jnp.where(p == beside, 0.25, 0.0)
    i = sublanes((EROWS, 64))
    c = lanes((EROWS, 64))
    middle = 8 + i // 2
    beside = middle + 2 * (i % 2) - 1
    raise_ = jnp.where(c == middle, 0.75, 0.0) + jnp.where(c == beside, 0.25, 0.0)
    warm = coarse[0]

    def columns(k):
        window = turn(warm, 32 - 64 * k, 1)[:, 0:128]
        return jnp.dot(window, widen, precision=HI, preferred_element_type=F32)

    lane64 = lanes((64, 128))
    tiles = [columns(k) for k in range(4)]
    tiles.append(jnp.where(lane64 < 64, columns(4), columns(-1)))
    for k in range(5):
        temp[k] = jnp.dot(raise_, tiles[k], precision=HI, preferred_element_type=F32)

    factor = -4.0 * LOG2E
    for rows, source in ((top, above), (low, below)):
        tile = source[0:16, :]
        for f in range(6):
            field[f, 4, rows, :] = join_sides(f, tile, 0, tile, 64)
        cw[1, rows, :] = factor * join_sides(6, tile, 0, tile, 64)
        cw[0, rows, :] = jnp.broadcast_to(factor * tile[:, 60:61], (HROW, 128))
    for f in range(6):
        field[f, 4, mid, :] = side[f]
    cw[1, mid, :] = factor * side[6]
    cw[0, mid, :] = factor * mark_rows(weights, 0, ROWS)

    lane = lanes((8, 128))
    first = gx * ROWS - HROW + BAND * sublanes((8, 128))
    rest = pl.ds(COLS, 128)
    col = gy * COLS + jnp.where(lane < 64, lane + COLS, lane - 128)
    inner_col = (col >= 1) & (col < GY * COLS)
    for t in range(BAND):
        row = first + t
        inner_row = (row >= 1) & (row < GX * ROWS)
        own_rate = cw[0, strip_of(t), :]
        for k in range(4):
            rate[t, :, pl.ds(128 * k, 128)] = own_rate
        rate[t, :, rest] = cw[1, strip_of(t), :]
        for k in range(5):
            warmth[t, :, pl.ds(128 * k, 128)] = (0.5 * EXPANSION) * temp[k, strip_of(t), :]
        for f in range(4):
            state[f, t, :, rest] = field[f, 4, strip_of(t), :]
        state[4, t, :, rest] = jnp.where(inner_row, field[4, 4, strip_of(t), :], 0.0)
        state[5, t, :, rest] = jnp.where(inner_col, field[5, 4, strip_of(t), :], 0.0)
    before = turn(warmth[BAND - 1], 1, 0)
    for t in range(BAND):
        own = warmth[t]
        tx[t] = own + before
        ty[t] = own + turn(own, 1, 1)
        before = own
    fetch.wait()

    keep = 1.0 - TIME_STEP * DAMPING

    def edge_x(t, a0, a1, o0, o1):
        open_x = a0 - o0 - tx[t]
        stretch = jnp.maximum(open_x, 0.0)
        spring = jnp.minimum(state[4, t], jnp.exp2(rate[t] * (stretch * stretch)))
        state[4, t] = spring
        return spring * open_x, spring * (a1 - o1)

    def substep(_, carry):
        a0, a1 = state[0, BAND - 1], state[1, BAND - 1]
        first_nx, first_ax = edge_x(0, state[0, 0], state[1, 0], turn(a0, 1, 0), turn(a1, 1, 0))
        next_nx, next_ax = turn(first_nx, -1, 0), turn(first_ax, -1, 0)
        for t in reversed(range(BAND)):
            open_y = a1 - turn(a1, 1, 1) - ty[t]
            stretch = jnp.maximum(open_y, 0.0)
            spring = jnp.minimum(state[5, t], jnp.exp2(rate[t] * (stretch * stretch)))
            state[5, t] = spring
            ny = spring * open_y
            ay = spring * (a0 - turn(a0, 1, 1))
            if t > 0:
                o0, o1 = state[0, t - 1], state[1, t - 1]
                nx, ax = edge_x(t, a0, a1, o0, o1)
            else:
                o0, o1 = a0, a1
                nx, ax = first_nx, first_ax
            force0 = (next_nx - nx) + (turn(ay, -1, 1) - ay)
            force1 = (next_ax - ax) + (turn(ny, -1, 1) - ny)
            next_nx, next_ax = nx, ax
            b0 = keep * state[2, t] + TIME_STEP * force0
            b1 = keep * state[3, t] + TIME_STEP * force1
            state[2, t] = b0
            state[3, t] = b1
            state[0, t] = a0 + TIME_STEP * b0
            state[1, t] = a1 + TIME_STEP * b1
            a0, a1 = o0, o1
        return carry

    lax.fori_loop(0, SUBSTEPS, substep, 0)
    for f in range(6):
        for t in range(BAND):
            for k in range(4):
                field[f, k, pl.ds(t, 8, stride=BAND), :] = state[f, t, :, pl.ds(128 * k, 128)]
        if f == 3:
            start_all(results[:-1])
    for b in range(10):
        rows = pl.ds(8 + 8 * b, 8)
        row = gx * ROWS - 8 + 8 * b + sublanes((8, 128))
        for k in range(4):
            cols = pl.ds(128 * k, 128)
            dx = jnp.where(row >= 1, 1.0 - field[4, k, rows, :], 0.0)
            dy = 1.0 - field[5, k, rows, :]
            if k == 0:
                dy = jnp.where(gy * COLS + lane >= 1, dy, 0.0)
            gap[k, pl.ds(8 * b, 8), :] = dx + dy
            if 1 <= b < 9:
                worn[0, pl.ds(8 * b - 8, 8), cols] = dx.astype(jnp.bfloat16)
                worn[1, pl.ds(8 * b - 8, 8), cols] = dy.astype(jnp.bfloat16)
    start_all(results[-1:])
    pairs = [
        gap[k, pl.ds(0, HEAT_ROWS, stride=2), :] + gap[k, pl.ds(1, HEAT_ROWS, stride=2), :]
        for k in range(4)
    ]
    for k in range(2):
        resist_out[:, pl.ds(128 * k, 128)] = jnp.dot(
            jnp.concatenate(pairs[2 * k : 2 * k + 2], axis=1),
            table[...],
            precision=HI,
            preferred_element_type=F32,
        )
    edge_out[...] = resist_out[:, 128:256]
    conduct = (1.0 + 0.5 * coarse[0, 12 : 12 + HEAT_ROWS, 0:CCOLS]) / (1.0 + resist_out[...])
    shape = (HEAT_ROWS, CCOLS)
    row = gx * CROWS - 4 + sublanes(shape)
    down = jnp.where((row >= 1) & (row < GX * CROWS), 0.5 * (conduct + turn(conduct, 1, 0)), 0.0)
    side = jnp.where(lanes(shape) >= 1, 0.5 * (conduct + turn(conduct, 1, 1)), 0.0)
    offsum = (down + turn(down, -1, 0) + side + turn(side, -1, 1))[4 : 4 + CROWS]
    capacity = coarse[1, 16:48, 0:CCOLS]
    top = jnp.max(offsum / (capacity + offsum), axis=(0, 1), keepdims=True)
    a = sublanes((8, CCOLS))
    c = lanes((8, CCOLS))
    border = jnp.where(sublanes((8, CROWS)) >= 6, top, 0.0)
    for k, value in enumerate((offsum, capacity, conduct[4 : 4 + CROWS])):
        pick = jnp.where(
            ((a == 2 * k) & (c == 0)) | ((a == 2 * k + 1) & (c == CCOLS - 1)), 1.0, 0.0
        )
        border += lax.dot_general(
            pick,
            value,
            (((1,), (1,)), ((), ())),
            precision=HI,
            preferred_element_type=F32,
        )
    for g in range(GX):
        border_tiles[g] = jnp.zeros((8, 128), F32)
        border_tiles[g, :, 0:CROWS] = border
    send = pltpu.make_async_copy(border_tiles, tops_out, sem.at[10])
    send.start()
    wait_all(results + [send])


def conductances(resist, from_left, coarse):
    gx = lax.axis_index("gx")
    gy = lax.axis_index("gy")
    shape = (HEAT_ROWS, WCOLS)
    lane = lanes((HEAT_ROWS, 128))
    rim = jnp.where(lane < 64, 0.0, from_left[...])
    wide = jnp.concatenate([resist[...], rim], axis=1)
    warm = coarse[0]
    conduct = (1.0 + 0.5 * warm) / (1.0 + wide)
    row = gx * CROWS - 4 + sublanes(shape)
    lane = lanes(shape)
    col = gy * CCOLS + jnp.where(lane < CCOLS + 64, lane, lane - WCOLS)
    down = jnp.where(
        (row >= 1) & (row < GX * CROWS), 0.5 * (conduct + turn(conduct, 1, 0)), 0.0
    )
    side = jnp.where(
        (col >= 1) & (col < GY * CCOLS), 0.5 * (conduct + turn(conduct, 1, 1)), 0.0
    )
    up = turn(down, -1, 0)
    far = turn(side, -1, 1)
    offsum = down + up + side + far
    return warm, down, up, side, far, offsum, coarse[1] + offsum


def solve_kernel(resist, from_left, coarse, tops, out):
    warm, down, up, side, far, _, diagonal = conductances(resist, from_left, coarse)
    inverse = 1.0 / diagonal

    def spread(x):
        return (
            down * turn(x, 1, 0) + up * turn(x, -1, 0) + side * turn(x, 1, 1) + far * turn(x, -1, 1)
        ) * inverse

    start = coarse[2] + (
        down * (turn(warm, 1, 0) - warm)
        + up * (turn(warm, -1, 0) - warm)
        + side * (turn(warm, 1, 1) - warm)
        + far * (turn(warm, -1, 1) - warm)
    )
    z = start * inverse
    y = z + spread(z)
    y2 = turn(spread(spread(y)), 4, 1)
    y = turn(y, 4, 1)
    group = lanes((8, 128)) // 32
    strip = []
    for h in range(2):
        tile = tops[4 * h]
        for k in range(1, 4):
            tile = jnp.where(group == k, turn(tops[4 * h + k], 32 * k, 1), tile)
        strip.append(tile)
    last_y, last_y2 = y[:, CCOLS:], turn(y2[:, CCOLS:], 64, 1)
    tail = jnp.where(lanes(last_y.shape) < 64, last_y, last_y2)
    for g in range(GY):
        rows = slice(4 + 2 * g, 6 + 2 * g)
        for h in range(2):
            cols = slice(128 * h, 128 * h + 128)
            out[g, 2 * h : 2 * h + 2, :] = y[rows, cols]
            out[g, 4 + 2 * h : 6 + 2 * h, :] = y2[rows, cols]
            out[g, 8 + 8 * h : 16 + 8 * h, :] = strip[h]
            out[g, 15 + 8 * h : 16 + 8 * h, :] = tail[4 + 2 * g + h : 5 + 2 * g + h]


def finish_kernel(recv, warm, out, wide, border):
    for g in range(GY):
        for k in range(7):
            for h in range(2):
                border[k, g : g + 1, pl.ds(128 * h, 128)] = recv[g, 8 + 8 * h + k : 9 + 8 * h + k, :]
    across = 0.5 * (turn(border[5], 1, 0) + border[4])
    across = jnp.where(sublanes((GY, CCOLS)) >= 1, across, 0.0)
    top = border[6]
    for k, face in ((0, across), (1, turn(across, -1, 0))):
        offsum = border[k] + face
        top = jnp.maximum(top, offsum / (border[2 + k] + offsum))
    top = jnp.max(top, axis=(0, 1), keepdims=True)
    square = top * top
    gain = 8.0 / (8.0 - 8.0 * square + square * square)
    near = gain * (1.0 - square)
    for g in range(GY):
        for h in range(2):
            wide[:, pl.ds(CCOLS * g + 128 * h, 128)] = (
                near * recv[g, 2 * h : 2 * h + 2, :] + gain * recv[g, 4 + 2 * h : 6 + 2 * h, :]
            )
    for h in range(2):
        tail = recv[GY - 1, 15 + 8 * h : 16 + 8 * h, :]
        wide[h : h + 1, pl.ds(CCOLS * GY, 128)] = near * tail + gain * turn(tail, 64, 1)
    out[...] = warm[...] + turn(wide[...], -4, 1)[:, : GY * CCOLS]


def vmem(count):
    return [pl.BlockSpec(memory_space=pltpu.VMEM)] * count


ANY = pl.BlockSpec(memory_space=pl.ANY)
FAR = pl.BlockSpec(memory_space=pltpu.MemorySpace.HBM)
PARAMS = pltpu.CompilerParams(vmem_limit_bytes=32 * 1024 * 1024)


def shaped(*shape, dtype=F32):
    return jax.ShapeDtypeStruct(shape, dtype)


def ahead(axis):
    count = lax.axis_size(axis)
    return [(i, (i + 1) % count) for i in range(count)]


def neighbours(value_up, value_down, axis):
    back = [(j, i) for i, j in ahead(axis)]
    return lax.ppermute(value_up, axis, ahead(axis)), lax.ppermute(value_down, axis, back)


def exchange(value, axis):
    return lax.all_to_all(value, axis, split_axis=0, concat_axis=0, tiled=True)


def per_device(u, v, d, marks, warm, cap, film, bath):
    far = [
        pltpu.with_memory_space_constraint(x, pltpu.MemorySpace.HBM)
        for x in (marks.reshape(ROWS // 8), u, v, d, warm, cap, film, bath)
    ]
    side = pltpu.VMEM((2, 2, ROWS, 128), F32)
    line = pltpu.VMEM((2, GY * CCOLS), F32)
    packed, weights = pl.pallas_call(
        pack_kernel,
        out_shape=(shaped(GY, CHUNK, 128), shaped(8, 128)),
        in_specs=[FAR] * 8,
        out_specs=tuple(vmem(2)),
        scratch_shapes=[pltpu.SMEM((ROWS // 8,), jnp.int32)]
        + [side, side, pltpu.VMEM((2, 2, ROWS, 128), jnp.int32)]
        + [line] * 4
        + [pltpu.VMEM((8, GY * CCOLS), F32), pltpu.SemaphoreType.DMA((11,))],
        compiler_params=PARAMS,
        name="pack",
    )(*far)
    recv = exchange(packed, "gy")
    up_rows, down_rows = pl.pallas_call(
        rows_kernel,
        out_shape=(shaped(6, 4, HROW, 128), shaped(6, 4, HROW, 128)),
        in_specs=vmem(1) + [FAR] * 3,
        out_specs=tuple(vmem(2)),
        scratch_shapes=[
            pltpu.VMEM((2, 2, HROW, COLS), jnp.int32),
            pltpu.SemaphoreType.DMA((18,)),
        ],
        compiler_params=PARAMS,
        name="rows",
    )(weights, *far[1:4])
    above_rows, below_rows = neighbours(up_rows, down_rows, "gx")
    up, down = pl.pallas_call(
        rim_kernel,
        out_shape=(shaped(CORNER, 128), shaped(CORNER, 128)),
        in_specs=vmem(2),
        out_specs=tuple(vmem(2)),
        compiler_params=PARAMS,
        name="rim",
    )(weights, recv)
    above, below = neighbours(up, down, "gx")
    state, side, coarse, table = pl.pallas_call(
        prep_kernel,
        out_shape=(
            shaped(6, BAND, 8, ECOLS),
            shaped(7, ROWS, 128),
            shaped(3, CROWS, WCOLS),
            shaped(256, 128),
        ),
        in_specs=vmem(1) + [ANY, ANY] + vmem(2) + [ANY, ANY],
        out_specs=tuple(vmem(4)),
        scratch_shapes=[
            pltpu.VMEM((6, 4, EROWS, 128), F32),
            pltpu.SemaphoreType.DMA((10,)),
        ],
        compiler_params=PARAMS,
        name="prep",
    )(weights, u, v, d, recv, above_rows, below_rows)
    band = pltpu.VMEM((BAND, 8, ECOLS), F32)
    shift, speed, damage, resist, coarse, edge, tops = pl.pallas_call(
        plate_kernel,
        out_shape=(
            shaped(2, ROWS, COLS),
            shaped(2, ROWS, COLS),
            shaped(2, ROWS, COLS, dtype=jnp.bfloat16),
            shaped(HEAT_ROWS, CCOLS),
            shaped(3, HEAT_ROWS, WCOLS),
            shaped(HEAT_ROWS, 128),
            shaped(GX, 8, 128),
        ),
        in_specs=vmem(1) + [ANY] + vmem(5),
        out_specs=(ANY, ANY, ANY) + tuple(vmem(3)) + (ANY,),
        scratch_shapes=[
            pltpu.VMEM((6, 5, EROWS, 128), F32),
            pltpu.VMEM((2, EROWS, 128), F32),
            pltpu.VMEM((5, EROWS, 128), F32),
            pltpu.VMEM((6, BAND, 8, ECOLS), F32),
            band,
            band,
            band,
            band,
            pltpu.VMEM((3, 64, WCOLS), F32),
            pltpu.VMEM((4, 2 * HEAT_ROWS, 128), F32),
            pltpu.VMEM((2, ROWS, COLS), jnp.bfloat16),
            pltpu.VMEM((GX, 8, 128), F32),
            pltpu.SemaphoreType.DMA((11,)),
        ],
        compiler_params=PARAMS,
        name="plate",
    )(weights, state, side, coarse, table, above, below)
    from_left = lax.ppermute(edge, "gy", ahead("gy"))
    tops = exchange(tops, "gx")
    answer = pl.pallas_call(
        solve_kernel,
        out_shape=shaped(GY, 24, 128),
        in_specs=vmem(4),
        out_specs=vmem(1)[0],
        compiler_params=PARAMS,
        name="solve",
    )(resist, from_left, coarse, tops)
    answer = exchange(answer, "gy")
    warmth = pl.pallas_call(
        finish_kernel,
        out_shape=shaped(2, GY * CCOLS),
        in_specs=vmem(2),
        out_specs=vmem(1)[0],
        scratch_shapes=[pltpu.VMEM((2, GY * CCOLS + 128), F32), pltpu.VMEM((7, GY, CCOLS), F32)],
        compiler_params=PARAMS,
        name="finish",
    )(answer, warm)
    return shift, speed, damage, warmth


def solution(mesh):
    tile = P(None, "gx", "gy")
    line = P(("gx", "gy"), None)
    return jax.shard_map(
        per_device,
        mesh=mesh,
        in_specs=(tile, tile, tile, P("gx", "gy"), line, line, line, line),
        out_specs=(tile, tile, tile, line),
        check_vma=False,
    )
```

```python
import jax
import jax.numpy as jnp
from jax import lax
from jax.experimental import pallas as pl
from jax.experimental.pallas import tpu as pltpu
from jax.sharding import PartitionSpec as P

F32 = jnp.float32
ROWS, COLS = 64, 512
CROWS, CCOLS = 32, 256
GX, GY = 8, 16
HALO = 8
HROW = 16
EROWS = ROWS + 2 * HROW
ECOLS = COLS + 128
WCOLS = CCOLS + 128
HEAT_ROWS = CROWS + 8
BAND = EROWS // 8
SUBSTEPS = 8
SEG = 128
TIME_STEP = 0.4
DAMPING = 0.05
EXPANSION = 0.6
LOG2E = 1.4426950408889634
HI = lax.Precision.HIGH
CHUNK = 56
CORNER = 16 + 48 + 24 + 24


def lanes(shape):
    return lax.broadcasted_iota(jnp.int32, shape, len(shape) - 1)


def sublanes(shape):
    return lax.broadcasted_iota(jnp.int32, shape, len(shape) - 2)


def turn(value, shift, axis):
    size = value.shape[axis]
    shift %= size
    return value if shift == 0 else pltpu.roll(value, shift, axis)


def mark_rows(weights, first, count):
    parts = [
        jnp.broadcast_to(weights[first // 8 + k : first // 8 + k + 1, :], (8, 128))
        for k in range(count // 8)
    ]
    return jnp.concatenate(parts, axis=0)


def start_all(copies):
    for copy in copies:
        copy.start()


def wait_all(copies):
    for copy in copies:
        copy.wait()


def pack_kernel(
    marks_hbm, u_hbm, v_hbm, d_hbm, warm_hbm, cap_hbm, film_hbm, bath_hbm,
    out, weights,
    marks, u, v, d, warm, cap, film, bath, lines, sem,
):
    pairs = [(marks_hbm, marks)]
    pairs += [(warm_hbm, warm), (cap_hbm, cap), (film_hbm, film), (bath_hbm, bath)]
    for far, near in ((u_hbm, u), (v_hbm, v), (d_hbm, d)):
        for side, at in ((0, 0), (1, COLS - 128)):
            pairs.append((far.at[:, :, pl.ds(at, 128)], near.at[side]))
    copies = [pltpu.make_async_copy(a, b, sem.at[k]) for k, (a, b) in enumerate(pairs)]
    start_all(copies)
    gy = lax.axis_index("gy")
    zero = jnp.zeros((32, 128), F32)
    for g in range(GY):
        out[g, 24:CHUNK, :] = zero
    wait_all(copies[:5])
    for k in range(ROWS // 8):
        weights[k : k + 1, :] = jnp.full((1, 128), marks[k].astype(F32), F32)
    lines[0:2, :] = warm[...]
    lines[2:4, :] = cap[...] + film[...]
    lines[4:6, :] = film[...] * (bath[...] - warm[...])
    lines[6:8, :] = jnp.zeros((2, GY * CCOLS), F32)
    lane = lanes((8, 128))
    for g in range(GY):
        at = g * CCOLS
        out[g, 0:8, :] = lines[:, at : at + 128]
        out[g, 8:16, :] = lines[:, at + 128 : at + 256]
        if g > 0:
            left = lines[:, at - 128 : at]
        else:
            left = jnp.broadcast_to(lines[:, 0:1], (8, 128))
        if g < GY - 1:
            right = lines[:, at + 256 : at + 384]
        else:
            right = jnp.broadcast_to(lines[:, GY * CCOLS - 1 : GY * CCOLS], (8, 128))
        out[g, 16:24, :] = jnp.where(lane < 64, right, left)
    wait_all(copies[5:])

    def edge(side, inner):
        wide = lanes((ROWS, 128))
        weight = mark_rows(weights, 0, ROWS)
        tiles = [u[side, 0], u[side, 1], v[side, 0], v[side, 1]]
        tiles += [1.0 - d[side, f].astype(F32) * (0.125 * weight) for f in range(2)]
        packed = jnp.zeros((ROWS, 128), F32)
        for f, tile in enumerate(tiles + [weight]):
            moved = turn(tile, 8 * f - inner, 1)
            packed = jnp.where((wide >= 8 * f) & (wide < 8 * f + 8), moved, packed)
        return packed[:32] + turn(packed[32:], 64, 1)

    @pl.when(gy < GY - 1)
    def _():
        out[gy + 1, 24:CHUNK, :] = edge(1, 120)

    @pl.when(gy > 0)
    def _():
        out[gy - 1, 24:CHUNK, :] = edge(0, 0)


def rows_kernel(weights, u_hbm, v_hbm, d_hbm, up, down, d, sem):
    copies, levels = [], []
    for m, (message, row0) in enumerate(((up, ROWS - HROW), (down, 0))):
        rows = pl.ds(row0, HROW)
        for k in range(4):
            cols = pl.ds(128 * k, 128)
            for f, far in enumerate((u_hbm, v_hbm)):
                copies.append(
                    pltpu.make_async_copy(
                        far.at[:, rows, cols],
                        message.at[2 * f : 2 * f + 2, k],
                        sem.at[8 * m + 2 * k + f],
                    )
                )
        levels.append(pltpu.make_async_copy(d_hbm.at[:, rows, :], d.at[m], sem.at[16 + m]))
    start_all(levels + copies)
    wait_all(levels)
    for m, (message, row0) in enumerate(((up, ROWS - HROW), (down, 0))):
        weight = 0.125 * mark_rows(weights, row0, HROW)
        for f in range(2):
            for k in range(4):
                level = d[m, f, :, pl.ds(128 * k, 128)].astype(F32)
                message[4 + f, k] = 1.0 - level * weight
    wait_all(copies)


def join_sides(f, left, left_at, right, right_at):
    lane = lanes(left.shape)
    from_right = turn(right, -(right_at + 8 * f), 1)
    from_left = turn(left, 120 - left_at - 8 * f, 1)
    return jnp.where(lane < 8, from_right, jnp.where(lane >= 120, from_left, 0.0))


def sides(recv):
    gy = lax.axis_index("gy")
    left = recv[jnp.maximum(gy - 1, 0), 24:CHUNK, :]
    right = recv[jnp.minimum(gy + 1, GY - 1), 24:CHUNK, :]
    return left, right


def rim_kernel(weights, recv, up, down):
    left, right = sides(recv)
    lane = lanes((HROW, 128))
    for out, row0, coarse0, thin0 in ((up, ROWS - HROW, 16, 24), (down, 0, 0, 0)):
        if row0 == 0:
            near, off = left[0:16], turn(right[0:16], 64, 1)
        else:
            near, off = turn(left[16:32], 64, 1), right[16:32]
        corner = jnp.where(lane < 56, near, off)
        out[0:16, :] = jnp.where(
            (lane >= 56) & (lane < 64), mark_rows(weights, row0, HROW), corner
        )
        for k in range(3):
            for r in range(0, 16, 2):
                g = (coarse0 + r) // 2
                out[16 + 16 * k + r : 18 + 16 * k + r, :] = recv[g, 8 * k : 8 * k + 2, :]
            for r in range(0, 8, 2):
                g = (thin0 + r) // 2
                for a, base in ((1, 64), (2, 88)):
                    out[base + 8 * k + r : base + 8 * k + r + 2, :] = recv[
                        g, 8 * k + 2 * a : 8 * k + 2 * a + 2, :
                    ]


def strip_of(t):
    return pl.ds(t, 8, stride=BAND)


def prep_kernel(
    weights, u, v, d, recv, above_rows, below_rows,
    state, side, coarse, table,
    field, sem,
):
    gx = lax.axis_index("gx")
    gy = lax.axis_index("gy")
    top = pl.ds(0, HROW)
    mid = pl.ds(HROW, ROWS)
    low = pl.ds(HROW + ROWS, HROW)
    copies = [
        pltpu.make_async_copy(above_rows, field.at[:, :, top], sem.at[0]),
        pltpu.make_async_copy(below_rows, field.at[:, :, low], sem.at[1]),
    ]
    for k in range(4):
        cols = pl.ds(128 * k, 128)
        for f, source in enumerate((u, v)):
            here = field.at[2 * f : 2 * f + 2, k, mid]
            copies.append(pltpu.make_async_copy(source.at[:, :, cols], here, sem.at[2 + 2 * k + f]))
    start_all(copies)
    left, right = sides(recv)
    for k in range(3):
        cols = pl.ds(128 * k, 128)
        for g in range(GY):
            for a in range(3):
                coarse[a, 2 * g : 2 * g + 2, cols] = recv[g, 8 * k + 2 * a : 8 * k + 2 * a + 2, :]
    p = sublanes((256, 128))
    q = lanes((256, 128))
    place = (p % SEG).astype(F32)
    even = (2 * (q % 64)).astype(F32)
    spread = jnp.exp(jnp.abs(place - even) * (-4.0 / SEG)) + jnp.exp(
        jnp.abs(place - even - 1.0) * (-4.0 / SEG)
    )
    table[...] = jnp.where(p // SEG == q // 64, spread * (0.5 * 2.0 / SEG), 0.0)
    for f in range(7):
        for half in (0, 32):
            side[f, pl.ds(half, 32), :] = join_sides(
                f, left, half * 2, right, half * 2
            )
    weight = 0.125 * mark_rows(weights, 0, ROWS)
    for f in range(2):
        for k in range(4):
            level = d[f, :, pl.ds(128 * k, 128)].astype(F32)
            field[4 + f, k, mid, :] = 1.0 - level * weight
    wait_all(copies)
    lane = lanes((8, 128))
    first = gx * ROWS - HROW + BAND * sublanes((8, 128))
    for t in range(BAND):
        row = first + t
        inner_row = (row >= 1) & (row < GX * ROWS)
        for k in range(4):
            cols = pl.ds(128 * k, 128)
            for f in range(4):
                state[f, t, :, cols] = field[f, k, strip_of(t), :]
            state[4, t, :, cols] = jnp.where(inner_row, field[4, k, strip_of(t), :], 0.0)
            spring = field[5, k, strip_of(t), :]
            if k == 0:
                spring = jnp.where(gy * COLS + lane >= 1, spring, 0.0)
            state[5, t, :, cols] = spring


def plate_kernel(
    weights, state_in, side, coarse_in, table, above, below,
    shift_out, speed_out, damage_out, resist_out, coarse_out, edge_out, tops_out,
    field, cw, temp, state, rate, warmth, tx, ty, coarse, gap, worn, border_tiles, sem,
):
    gx = lax.axis_index("gx")
    gy = lax.axis_index("gy")
    top = pl.ds(0, HROW)
    mid = pl.ds(HROW, ROWS)
    low = pl.ds(HROW + ROWS, HROW)
    main = pl.ds(0, COLS)
    fetch = pltpu.make_async_copy(
        state_in.at[:, :, :, main], state.at[:, :, :, main], sem.at[9]
    )
    fetch.start()
    results = []
    for k in range(4):
        cols = pl.ds(128 * k, 128)
        for f, target in enumerate((shift_out, speed_out)):
            here = field.at[2 * f : 2 * f + 2, k, mid]
            results.append(
                pltpu.make_async_copy(here, target.at[:, :, cols], sem.at[2 * k + f])
            )
    results.append(pltpu.make_async_copy(worn, damage_out, sem.at[8]))

    coarse[:, 16:48, :] = coarse_in[...]
    for k in range(3):
        cols = pl.ds(128 * k, 128)
        coarse[0, 0:16, cols] = above[16 + 16 * k : 32 + 16 * k, :]
        coarse[0, 48:64, cols] = below[16 + 16 * k : 32 + 16 * k, :]
        for a, base in ((1, 64), (2, 88)):
            coarse[a, 8:16, cols] = above[base + 8 * k : base + 8 * k + 8, :]
            coarse[a, 48:56, cols] = below[base + 8 * k : base + 8 * k + 8, :]

    @pl.when(gx == 0)
    def _():
        coarse[0, 0:16, :] = jnp.broadcast_to(coarse[0, 16:17, :], (16, WCOLS))
        coarse[1, 8:16, :] = jnp.ones((8, WCOLS), F32)

    @pl.when(gx == GX - 1)
    def _():
        coarse[0, 48:64, :] = jnp.broadcast_to(coarse[0, 47:48, :], (16, WCOLS))
        coarse[1, 48:56, :] = jnp.ones((8, WCOLS), F32)

    coarse_out[...] = coarse[:, 12 : 12 + HEAT_ROWS, :]

    p = sublanes((128, 128))
    q = lanes((128, 128))
    middle = 32 + q // 2
    beside = middle + 2 * (q % 2) - 1
    widen = jnp.where(p == middle, 0.75, 0.0) + jnp.where(p == beside, 0.25, 0.0)
    i = sublanes((EROWS, 64))
    c = lanes((EROWS, 64))
    middle = 8 + i // 2
    beside = middle + 2 * (i % 2) - 1
    raise_ = jnp.where(c == middle, 0.75, 0.0) + jnp.where(c == beside, 0.25, 0.0)
    warm = coarse[0]

    def columns(k):
        window = turn(warm, 32 - 64 * k, 1)[:, 0:128]
        return jnp.dot(window, widen, precision=HI, preferred_element_type=F32)

    lane64 = lanes((64, 128))
    tiles = [columns(k) for k in range(4)]
    tiles.append(jnp.where(lane64 < 64, columns(4), columns(-1)))
    for k in range(5):
        temp[k] = jnp.dot(raise_, tiles[k], precision=HI, preferred_element_type=F32)

    factor = -4.0 * LOG2E
    for rows, source in ((top, above), (low, below)):
        tile = source[0:16, :]
        for f in range(6):
            field[f, 4, rows, :] = join_sides(f, tile, 0, tile, 64)
        cw[1, rows, :] = factor * join_sides(6, tile, 0, tile, 64)
        cw[0, rows, :] = jnp.broadcast_to(factor * tile[:, 60:61], (HROW, 128))
    for f in range(6):
        field[f, 4, mid, :] = side[f]
    cw[1, mid, :] = factor * side[6]
    cw[0, mid, :] = factor * mark_rows(weights, 0, ROWS)

    lane = lanes((8, 128))
    first = gx * ROWS - HROW + BAND * sublanes((8, 128))
    rest = pl.ds(COLS, 128)
    col = gy * COLS + jnp.where(lane < 64, lane + COLS, lane - 128)
    inner_col = (col >= 1) & (col < GY * COLS)
    for t in range(BAND):
        row = first + t
        inner_row = (row >= 1) & (row < GX * ROWS)
        own_rate = cw[0, strip_of(t), :]
        for k in range(4):
            rate[t, :, pl.ds(128 * k, 128)] = own_rate
        rate[t, :, rest] = cw[1, strip_of(t), :]
        for k in range(5):
            warmth[t, :, pl.ds(128 * k, 128)] = (0.5 * EXPANSION) * temp[k, strip_of(t), :]
        for f in range(4):
            state[f, t, :, rest] = field[f, 4, strip_of(t), :]
        state[4, t, :, rest] = jnp.where(inner_row, field[4, 4, strip_of(t), :], 0.0)
        state[5, t, :, rest] = jnp.where(inner_col, field[5, 4, strip_of(t), :], 0.0)
    before = turn(warmth[BAND - 1], 1, 0)
    for t in range(BAND):
        own = warmth[t]
        tx[t] = own + before
        ty[t] = own + turn(own, 1, 1)
        before = own
    fetch.wait()

    keep = 1.0 - TIME_STEP * DAMPING

    def edge_x(t, a0, a1, o0, o1):
        open_x = a0 - o0 - tx[t]
        stretch = jnp.maximum(open_x, 0.0)
        spring = jnp.minimum(state[4, t], jnp.exp2(rate[t] * (stretch * stretch)))
        state[4, t] = spring
        return spring * open_x, spring * (a1 - o1)

    def substep(_, carry):
        a0, a1 = state[0, BAND - 1], state[1, BAND - 1]
        first_nx, first_ax = edge_x(0, state[0, 0], state[1, 0], turn(a0, 1, 0), turn(a1, 1, 0))
        next_nx, next_ax = turn(first_nx, -1, 0), turn(first_ax, -1, 0)
        for t in reversed(range(BAND)):
            open_y = a1 - turn(a1, 1, 1) - ty[t]
            stretch = jnp.maximum(open_y, 0.0)
            spring = jnp.minimum(state[5, t], jnp.exp2(rate[t] * (stretch * stretch)))
            state[5, t] = spring
            ny = spring * open_y
            ay = spring * (a0 - turn(a0, 1, 1))
            if t > 0:
                o0, o1 = state[0, t - 1], state[1, t - 1]
                nx, ax = edge_x(t, a0, a1, o0, o1)
            else:
                o0, o1 = a0, a1
                nx, ax = first_nx, first_ax
            force0 = (next_nx - nx) + (turn(ay, -1, 1) - ay)
            force1 = (next_ax - ax) + (turn(ny, -1, 1) - ny)
            next_nx, next_ax = nx, ax
            b0 = keep * state[2, t] + TIME_STEP * force0
            b1 = keep * state[3, t] + TIME_STEP * force1
            state[2, t] = b0
            state[3, t] = b1
            state[0, t] = a0 + TIME_STEP * b0
            state[1, t] = a1 + TIME_STEP * b1
            a0, a1 = o0, o1
        return carry

    lax.fori_loop(0, SUBSTEPS, substep, 0)
    for f in range(6):
        for t in range(BAND):
            for k in range(4):
                field[f, k, pl.ds(t, 8, stride=BAND), :] = state[f, t, :, pl.ds(128 * k, 128)]
        if f == 3:
            start_all(results[:-1])
    for b in range(10):
        rows = pl.ds(8 + 8 * b, 8)
        row = gx * ROWS - 8 + 8 * b + sublanes((8, 128))
        for k in range(4):
            cols = pl.ds(128 * k, 128)
            dx = jnp.where(row >= 1, 1.0 - field[4, k, rows, :], 0.0)
            dy = 1.0 - field[5, k, rows, :]
            if k == 0:
                dy = jnp.where(gy * COLS + lane >= 1, dy, 0.0)
            gap[k, pl.ds(8 * b, 8), :] = dx + dy
            if 1 <= b < 9:
                worn[0, pl.ds(8 * b - 8, 8), cols] = dx.astype(jnp.bfloat16)
                worn[1, pl.ds(8 * b - 8, 8), cols] = dy.astype(jnp.bfloat16)
    start_all(results[-1:])
    pairs = [
        gap[k, pl.ds(0, HEAT_ROWS, stride=2), :] + gap[k, pl.ds(1, HEAT_ROWS, stride=2), :]
        for k in range(4)
    ]
    for k in range(2):
        resist_out[:, pl.ds(128 * k, 128)] = jnp.dot(
            jnp.concatenate(pairs[2 * k : 2 * k + 2], axis=1),
            table[...],
            precision=HI,
            preferred_element_type=F32,
        )
    edge_out[...] = resist_out[:, 128:256]
    conduct = (1.0 + 0.5 * coarse[0, 12 : 12 + HEAT_ROWS, 0:CCOLS]) / (1.0 + resist_out[...])
    shape = (HEAT_ROWS, CCOLS)
    row = gx * CROWS - 4 + sublanes(shape)
    down = jnp.where((row >= 1) & (row < GX * CROWS), 0.5 * (conduct + turn(conduct, 1, 0)), 0.0)
    side = jnp.where(lanes(shape) >= 1, 0.5 * (conduct + turn(conduct, 1, 1)), 0.0)
    offsum = (down + turn(down, -1, 0) + side + turn(side, -1, 1))[4 : 4 + CROWS]
    capacity = coarse[1, 16:48, 0:CCOLS]
    top = jnp.max(offsum / (capacity + offsum), axis=(0, 1), keepdims=True)
    a = sublanes((8, CCOLS))
    c = lanes((8, CCOLS))
    border = jnp.where(sublanes((8, CROWS)) >= 6, top, 0.0)
    for k, value in enumerate((offsum, capacity, conduct[4 : 4 + CROWS])):
        pick = jnp.where(
            ((a == 2 * k) & (c == 0)) | ((a == 2 * k + 1) & (c == CCOLS - 1)), 1.0, 0.0
        )
        border += lax.dot_general(
            pick,
            value,
            (((1,), (1,)), ((), ())),
            precision=HI,
            preferred_element_type=F32,
        )
    for g in range(GX):
        border_tiles[g] = jnp.zeros((8, 128), F32)
        border_tiles[g, :, 0:CROWS] = border
    send = pltpu.make_async_copy(border_tiles, tops_out, sem.at[10])
    send.start()
    wait_all(results + [send])


def conductances(resist, from_left, coarse):
    gx = lax.axis_index("gx")
    gy = lax.axis_index("gy")
    shape = (HEAT_ROWS, WCOLS)
    lane = lanes((HEAT_ROWS, 128))
    rim = jnp.where(lane < 64, 0.0, from_left[...])
    wide = jnp.concatenate([resist[...], rim], axis=1)
    warm = coarse[0]
    conduct = (1.0 + 0.5 * warm) / (1.0 + wide)
    row = gx * CROWS - 4 + sublanes(shape)
    lane = lanes(shape)
    col = gy * CCOLS + jnp.where(lane < CCOLS + 64, lane, lane - WCOLS)
    down = jnp.where(
        (row >= 1) & (row < GX * CROWS), 0.5 * (conduct + turn(conduct, 1, 0)), 0.0
    )
    side = jnp.where(
        (col >= 1) & (col < GY * CCOLS), 0.5 * (conduct + turn(conduct, 1, 1)), 0.0
    )
    up = turn(down, -1, 0)
    far = turn(side, -1, 1)
    offsum = down + up + side + far
    return warm, down, up, side, far, offsum, coarse[1] + offsum


def solve_kernel(resist, from_left, coarse, tops, out):
    warm, down, up, side, far, _, diagonal = conductances(resist, from_left, coarse)
    inverse = 1.0 / diagonal

    def spread(x):
        return (
            down * turn(x, 1, 0) + up * turn(x, -1, 0) + side * turn(x, 1, 1) + far * turn(x, -1, 1)
        ) * inverse

    start = coarse[2] + (
        down * (turn(warm, 1, 0) - warm)
        + up * (turn(warm, -1, 0) - warm)
        + side * (turn(warm, 1, 1) - warm)
        + far * (turn(warm, -1, 1) - warm)
    )
    z = start * inverse
    y = z + spread(z)
    y2 = turn(spread(spread(y)), 4, 1)
    y = turn(y, 4, 1)
    group = lanes((8, 128)) // 32
    strip = []
    for h in range(2):
        tile = tops[4 * h]
        for k in range(1, 4):
            tile = jnp.where(group == k, turn(tops[4 * h + k], 32 * k, 1), tile)
        strip.append(tile)
    last_y, last_y2 = y[:, CCOLS:], turn(y2[:, CCOLS:], 64, 1)
    tail = jnp.where(lanes(last_y.shape) < 64, last_y, last_y2)
    for g in range(GY):
        rows = slice(4 + 2 * g, 6 + 2 * g)
        for h in range(2):
            cols = slice(128 * h, 128 * h + 128)
            out[g, 2 * h : 2 * h + 2, :] = y[rows, cols]
            out[g, 4 + 2 * h : 6 + 2 * h, :] = y2[rows, cols]
            out[g, 8 + 8 * h : 16 + 8 * h, :] = strip[h]
            out[g, 15 + 8 * h : 16 + 8 * h, :] = tail[4 + 2 * g + h : 5 + 2 * g + h]


def finish_kernel(recv, warm, out, wide, border):
    for g in range(GY):
        for k in range(7):
            for h in range(2):
                border[k, g : g + 1, pl.ds(128 * h, 128)] = recv[g, 8 + 8 * h + k : 9 + 8 * h + k, :]
    across = 0.5 * (turn(border[5], 1, 0) + border[4])
    across = jnp.where(sublanes((GY, CCOLS)) >= 1, across, 0.0)
    top = border[6]
    for k, face in ((0, across), (1, turn(across, -1, 0))):
        offsum = border[k] + face
        top = jnp.maximum(top, offsum / (border[2 + k] + offsum))
    top = jnp.max(top, axis=(0, 1), keepdims=True)
    square = top * top
    gain = 8.0 / (8.0 - 8.0 * square + square * square)
    near = gain * (1.0 - square)
    for g in range(GY):
        for h in range(2):
            wide[:, pl.ds(CCOLS * g + 128 * h, 128)] = (
                near * recv[g, 2 * h : 2 * h + 2, :] + gain * recv[g, 4 + 2 * h : 6 + 2 * h, :]
            )
    for h in range(2):
        tail = recv[GY - 1, 15 + 8 * h : 16 + 8 * h, :]
        wide[h : h + 1, pl.ds(CCOLS * GY, 128)] = near * tail + gain * turn(tail, 64, 1)
    out[...] = warm[...] + turn(wide[...], -4, 1)[:, : GY * CCOLS]


def vmem(count):
    return [pl.BlockSpec(memory_space=pltpu.VMEM)] * count


ANY = pl.BlockSpec(memory_space=pl.ANY)
FAR = pl.BlockSpec(memory_space=pltpu.MemorySpace.HBM)
PARAMS = pltpu.CompilerParams(vmem_limit_bytes=32 * 1024 * 1024)


def shaped(*shape, dtype=F32):
    return jax.ShapeDtypeStruct(shape, dtype)


def ahead(axis):
    count = lax.axis_size(axis)
    return [(i, (i + 1) % count) for i in range(count)]


def neighbours(value_up, value_down, axis):
    back = [(j, i) for i, j in ahead(axis)]
    return lax.ppermute(value_up, axis, ahead(axis)), lax.ppermute(value_down, axis, back)


def exchange(value, axis):
    return lax.all_to_all(value, axis, split_axis=0, concat_axis=0, tiled=True)


def per_device(u, v, d, marks, warm, cap, film, bath):
    far = [
        pltpu.with_memory_space_constraint(x, pltpu.MemorySpace.HBM)
        for x in (marks.reshape(ROWS // 8), u, v, d, warm, cap, film, bath)
    ]
    side = pltpu.VMEM((2, 2, ROWS, 128), F32)
    line = pltpu.VMEM((2, GY * CCOLS), F32)
    packed, weights = pl.pallas_call(
        pack_kernel,
        out_shape=(shaped(GY, CHUNK, 128), shaped(8, 128)),
        in_specs=[FAR] * 8,
        out_specs=tuple(vmem(2)),
        scratch_shapes=[pltpu.SMEM((ROWS // 8,), jnp.int32)]
        + [side, side, pltpu.VMEM((2, 2, ROWS, 128), jnp.int32)]
        + [line] * 4
        + [pltpu.VMEM((8, GY * CCOLS), F32), pltpu.SemaphoreType.DMA((11,))],
        compiler_params=PARAMS,
        name="pack",
    )(*far)
    recv = exchange(packed, "gy")
    up_rows, down_rows = pl.pallas_call(
        rows_kernel,
        out_shape=(shaped(6, 4, HROW, 128), shaped(6, 4, HROW, 128)),
        in_specs=vmem(1) + [FAR] * 3,
        out_specs=tuple(vmem(2)),
        scratch_shapes=[
            pltpu.VMEM((2, 2, HROW, COLS), jnp.int32),
            pltpu.SemaphoreType.DMA((18,)),
        ],
        compiler_params=PARAMS,
        name="rows",
    )(weights, *far[1:4])
    above_rows, below_rows = neighbours(up_rows, down_rows, "gx")
    up, down = pl.pallas_call(
        rim_kernel,
        out_shape=(shaped(CORNER, 128), shaped(CORNER, 128)),
        in_specs=vmem(2),
        out_specs=tuple(vmem(2)),
        compiler_params=PARAMS,
        name="rim",
    )(weights, recv)
    above, below = neighbours(up, down, "gx")
    state, side, coarse, table = pl.pallas_call(
        prep_kernel,
        out_shape=(
            shaped(6, BAND, 8, ECOLS),
            shaped(7, ROWS, 128),
            shaped(3, CROWS, WCOLS),
            shaped(256, 128),
        ),
        in_specs=vmem(1) + [ANY, ANY] + vmem(2) + [ANY, ANY],
        out_specs=tuple(vmem(4)),
        scratch_shapes=[
            pltpu.VMEM((6, 4, EROWS, 128), F32),
            pltpu.SemaphoreType.DMA((10,)),
        ],
        compiler_params=PARAMS,
        name="prep",
    )(weights, u, v, d, recv, above_rows, below_rows)
    band = pltpu.VMEM((BAND, 8, ECOLS), F32)
    shift, speed, damage, resist, coarse, edge, tops = pl.pallas_call(
        plate_kernel,
        out_shape=(
            shaped(2, ROWS, COLS),
            shaped(2, ROWS, COLS),
            shaped(2, ROWS, COLS, dtype=jnp.bfloat16),
            shaped(HEAT_ROWS, CCOLS),
            shaped(3, HEAT_ROWS, WCOLS),
            shaped(HEAT_ROWS, 128),
            shaped(GX, 8, 128),
        ),
        in_specs=vmem(1) + [ANY] + vmem(5),
        out_specs=(ANY, ANY, ANY) + tuple(vmem(3)) + (ANY,),
        scratch_shapes=[
            pltpu.VMEM((6, 5, EROWS, 128), F32),
            pltpu.VMEM((2, EROWS, 128), F32),
            pltpu.VMEM((5, EROWS, 128), F32),
            pltpu.VMEM((6, BAND, 8, ECOLS), F32),
            band,
            band,
            band,
            band,
            pltpu.VMEM((3, 64, WCOLS), F32),
            pltpu.VMEM((4, 2 * HEAT_ROWS, 128), F32),
            pltpu.VMEM((2, ROWS, COLS), jnp.bfloat16),
            pltpu.VMEM((GX, 8, 128), F32),
            pltpu.SemaphoreType.DMA((11,)),
        ],
        compiler_params=PARAMS,
        name="plate",
    )(weights, state, side, coarse, table, above, below)
    from_left = lax.ppermute(edge, "gy", ahead("gy"))
    tops = exchange(tops, "gx")
    answer = pl.pallas_call(
        solve_kernel,
        out_shape=shaped(GY, 24, 128),
        in_specs=vmem(4),
        out_specs=vmem(1)[0],
        compiler_params=PARAMS,
        name="solve",
    )(resist, from_left, coarse, tops)
    answer = exchange(answer, "gy")
    warmth = pl.pallas_call(
        finish_kernel,
        out_shape=shaped(2, GY * CCOLS),
        in_specs=vmem(2),
        out_specs=vmem(1)[0],
        scratch_shapes=[pltpu.VMEM((2, GY * CCOLS + 128), F32), pltpu.VMEM((7, GY, CCOLS), F32)],
        compiler_params=PARAMS,
        name="finish",
    )(answer, warm)
    return shift, speed, damage, warmth


def solution(mesh):
    tile = P(None, "gx", "gy")
    line = P(("gx", "gy"), None)
    return jax.shard_map(
        per_device,
        mesh=mesh,
        in_specs=(tile, tile, tile, P("gx", "gy"), line, line, line, line),
        out_specs=(tile, tile, tile, line),
        check_vma=False,
    )
```

```python
import jax
import jax.numpy as jnp
from jax import lax
from jax.experimental import pallas as pl
from jax.experimental.pallas import tpu as pltpu
from jax.sharding import PartitionSpec as P

F32 = jnp.float32
ROWS, COLS = 64, 512
CROWS, CCOLS = 32, 256
GX, GY = 8, 16
HALO = 8
HROW = 16
EROWS = ROWS + 2 * HROW
ECOLS = COLS + 128
WCOLS = CCOLS + 128
HEAT_ROWS = CROWS + 8
BAND = EROWS // 8
SUBSTEPS = 8
SEG = 128
TIME_STEP = 0.4
DAMPING = 0.05
EXPANSION = 0.6
LOG2E = 1.4426950408889634
HI = lax.Precision.HIGH
CHUNK = 56
CORNER = 16 + 48 + 24 + 24


def lanes(shape):
    return lax.broadcasted_iota(jnp.int32, shape, len(shape) - 1)


def sublanes(shape):
    return lax.broadcasted_iota(jnp.int32, shape, len(shape) - 2)


def turn(value, shift, axis):
    size = value.shape[axis]
    shift %= size
    return value if shift == 0 else pltpu.roll(value, shift, axis)


def mark_rows(weights, first, count):
    parts = [
        jnp.broadcast_to(weights[first // 8 + k : first // 8 + k + 1, :], (8, 128))
        for k in range(count // 8)
    ]
    return jnp.concatenate(parts, axis=0)


def start_all(copies):
    for copy in copies:
        copy.start()


def wait_all(copies):
    for copy in copies:
        copy.wait()


def pack_kernel(
    marks_hbm, u_hbm, v_hbm, d_hbm, warm_hbm, cap_hbm, film_hbm, bath_hbm,
    out, weights,
    marks, u, v, d, warm, cap, film, bath, lines, sem,
):
    pairs = [(marks_hbm, marks)]
    pairs += [(warm_hbm, warm), (cap_hbm, cap), (film_hbm, film), (bath_hbm, bath)]
    for far, near in ((u_hbm, u), (v_hbm, v), (d_hbm, d)):
        for side, at in ((0, 0), (1, COLS - 128)):
            pairs.append((far.at[:, :, pl.ds(at, 128)], near.at[side]))
    copies = [pltpu.make_async_copy(a, b, sem.at[k]) for k, (a, b) in enumerate(pairs)]
    start_all(copies)
    gy = lax.axis_index("gy")
    zero = jnp.zeros((32, 128), F32)
    for g in range(GY):
        out[g, 24:CHUNK, :] = zero
    wait_all(copies[:5])
    for k in range(ROWS // 8):
        weights[k : k + 1, :] = jnp.full((1, 128), marks[k].astype(F32), F32)
    lines[0:2, :] = warm[...]
    lines[2:4, :] = cap[...] + film[...]
    lines[4:6, :] = film[...] * (bath[...] - warm[...])
    lines[6:8, :] = jnp.zeros((2, GY * CCOLS), F32)
    lane = lanes((8, 128))
    for g in range(GY):
        at = g * CCOLS
        out[g, 0:8, :] = lines[:, at : at + 128]
        out[g, 8:16, :] = lines[:, at + 128 : at + 256]
        if g > 0:
            left = lines[:, at - 128 : at]
        else:
            left = jnp.broadcast_to(lines[:, 0:1], (8, 128))
        if g < GY - 1:
            right = lines[:, at + 256 : at + 384]
        else:
            right = jnp.broadcast_to(lines[:, GY * CCOLS - 1 : GY * CCOLS], (8, 128))
        out[g, 16:24, :] = jnp.where(lane < 64, right, left)
    wait_all(copies[5:])

    def edge(side, inner):
        wide = lanes((ROWS, 128))
        weight = mark_rows(weights, 0, ROWS)
        tiles = [u[side, 0], u[side, 1], v[side, 0], v[side, 1]]
        tiles += [1.0 - d[side, f].astype(F32) * (0.125 * weight) for f in range(2)]
        packed = jnp.zeros((ROWS, 128), F32)
        for f, tile in enumerate(tiles + [weight]):
            moved = turn(tile, 8 * f - inner, 1)
            packed = jnp.where((wide >= 8 * f) & (wide < 8 * f + 8), moved, packed)
        return packed[:32] + turn(packed[32:], 64, 1)

    @pl.when(gy < GY - 1)
    def _():
        out[gy + 1, 24:CHUNK, :] = edge(1, 120)

    @pl.when(gy > 0)
    def _():
        out[gy - 1, 24:CHUNK, :] = edge(0, 0)


def rows_kernel(weights, u_hbm, v_hbm, d_hbm, up, down, d, sem):
    copies, levels = [], []
    for m, (message, row0) in enumerate(((up, ROWS - HROW), (down, 0))):
        rows = pl.ds(row0, HROW)
        for k in range(4):
            cols = pl.ds(128 * k, 128)
            for f, far in enumerate((u_hbm, v_hbm)):
                copies.append(
                    pltpu.make_async_copy(
                        far.at[:, rows, cols],
                        message.at[2 * f : 2 * f + 2, k],
                        sem.at[8 * m + 2 * k + f],
                    )
                )
        levels.append(pltpu.make_async_copy(d_hbm.at[:, rows, :], d.at[m], sem.at[16 + m]))
    start_all(levels + copies)
    wait_all(levels)
    for m, (message, row0) in enumerate(((up, ROWS - HROW), (down, 0))):
        weight = 0.125 * mark_rows(weights, row0, HROW)
        for f in range(2):
            for k in range(4):
                level = d[m, f, :, pl.ds(128 * k, 128)].astype(F32)
                message[4 + f, k] = 1.0 - level * weight
    wait_all(copies)


def join_sides(f, left, left_at, right, right_at):
    lane = lanes(left.shape)
    from_right = turn(right, -(right_at + 8 * f), 1)
    from_left = turn(left, 120 - left_at - 8 * f, 1)
    return jnp.where(lane < 8, from_right, jnp.where(lane >= 120, from_left, 0.0))


def sides(recv):
    gy = lax.axis_index("gy")
    left = recv[jnp.maximum(gy - 1, 0), 24:CHUNK, :]
    right = recv[jnp.minimum(gy + 1, GY - 1), 24:CHUNK, :]
    return left, right


def rim_kernel(weights, recv, up, down):
    left, right = sides(recv)
    lane = lanes((HROW, 128))
    for out, row0, coarse0, thin0 in ((up, ROWS - HROW, 16, 24), (down, 0, 0, 0)):
        if row0 == 0:
            near, off = left[0:16], turn(right[0:16], 64, 1)
        else:
            near, off = turn(left[16:32], 64, 1), right[16:32]
        corner = jnp.where(lane < 56, near, off)
        out[0:16, :] = jnp.where(
            (lane >= 56) & (lane < 64), mark_rows(weights, row0, HROW), corner
        )
        for k in range(3):
            for r in range(0, 16, 2):
                g = (coarse0 + r) // 2
                out[16 + 16 * k + r : 18 + 16 * k + r, :] = recv[g, 8 * k : 8 * k + 2, :]
            for r in range(0, 8, 2):
                g = (thin0 + r) // 2
                for a, base in ((1, 64), (2, 88)):
                    out[base + 8 * k + r : base + 8 * k + r + 2, :] = recv[
                        g, 8 * k + 2 * a : 8 * k + 2 * a + 2, :
                    ]


def strip_of(t):
    return pl.ds(t, 8, stride=BAND)


def prep_kernel(
    weights, u, v, d, recv, above_rows, below_rows,
    state, side, coarse, table,
    field, sem,
):
    gx = lax.axis_index("gx")
    gy = lax.axis_index("gy")
    top = pl.ds(0, HROW)
    mid = pl.ds(HROW, ROWS)
    low = pl.ds(HROW + ROWS, HROW)
    copies = [
        pltpu.make_async_copy(above_rows, field.at[:, :, top], sem.at[0]),
        pltpu.make_async_copy(below_rows, field.at[:, :, low], sem.at[1]),
    ]
    for k in range(4):
        cols = pl.ds(128 * k, 128)
        for f, source in enumerate((u, v)):
            here = field.at[2 * f : 2 * f + 2, k, mid]
            copies.append(pltpu.make_async_copy(source.at[:, :, cols], here, sem.at[2 + 2 * k + f]))
    start_all(copies)
    left, right = sides(recv)
    for k in range(3):
        cols = pl.ds(128 * k, 128)
        for g in range(GY):
            for a in range(3):
                coarse[a, 2 * g : 2 * g + 2, cols] = recv[g, 8 * k + 2 * a : 8 * k + 2 * a + 2, :]
    p = sublanes((256, 128))
    q = lanes((256, 128))
    place = (p % SEG).astype(F32)
    even = (2 * (q % 64)).astype(F32)
    spread = jnp.exp(jnp.abs(place - even) * (-4.0 / SEG)) + jnp.exp(
        jnp.abs(place - even - 1.0) * (-4.0 / SEG)
    )
    table[...] = jnp.where(p // SEG == q // 64, spread * (0.5 * 2.0 / SEG), 0.0)
    for f in range(7):
        for half in (0, 32):
            side[f, pl.ds(half, 32), :] = join_sides(
                f, left, half * 2, right, half * 2
            )
    weight = 0.125 * mark_rows(weights, 0, ROWS)
    for f in range(2):
        for k in range(4):
            level = d[f, :, pl.ds(128 * k, 128)].astype(F32)
            field[4 + f, k, mid, :] = 1.0 - level * weight
    wait_all(copies)
    lane = lanes((8, 128))
    first = gx * ROWS - HROW + BAND * sublanes((8, 128))
    for t in range(BAND):
        row = first + t
        inner_row = (row >= 1) & (row < GX * ROWS)
        for k in range(4):
            cols = pl.ds(128 * k, 128)
            for f in range(4):
                state[f, t, :, cols] = field[f, k, strip_of(t), :]
            state[4, t, :, cols] = jnp.where(inner_row, field[4, k, strip_of(t), :], 0.0)
            spring = field[5, k, strip_of(t), :]
            if k == 0:
                spring = jnp.where(gy * COLS + lane >= 1, spring, 0.0)
            state[5, t, :, cols] = spring


def plate_kernel(
    weights, state_in, side, coarse_in, table, above, below,
    shift_out, speed_out, damage_out, resist_out, coarse_out, edge_out, tops_out,
    field, cw, temp, state, rate, warmth, tx, ty, coarse, gap, worn, border_tiles, sem,
):
    gx = lax.axis_index("gx")
    gy = lax.axis_index("gy")
    top = pl.ds(0, HROW)
    mid = pl.ds(HROW, ROWS)
    low = pl.ds(HROW + ROWS, HROW)
    main = pl.ds(0, COLS)
    fetch = pltpu.make_async_copy(
        state_in.at[:, :, :, main], state.at[:, :, :, main], sem.at[9]
    )
    fetch.start()
    results = []
    for k in range(4):
        cols = pl.ds(128 * k, 128)
        for f, target in enumerate((shift_out, speed_out)):
            here = field.at[2 * f : 2 * f + 2, k, mid]
            results.append(
                pltpu.make_async_copy(here, target.at[:, :, cols], sem.at[2 * k + f])
            )
    results.append(pltpu.make_async_copy(worn, damage_out, sem.at[8]))

    coarse[:, 16:48, :] = coarse_in[...]
    for k in range(3):
        cols = pl.ds(128 * k, 128)
        coarse[0, 0:16, cols] = above[16 + 16 * k : 32 + 16 * k, :]
        coarse[0, 48:64, cols] = below[16 + 16 * k : 32 + 16 * k, :]
        for a, base in ((1, 64), (2, 88)):
            coarse[a, 8:16, cols] = above[base + 8 * k : base + 8 * k + 8, :]
            coarse[a, 48:56, cols] = below[base + 8 * k : base + 8 * k + 8, :]

    @pl.when(gx == 0)
    def _():
        coarse[0, 0:16, :] = jnp.broadcast_to(coarse[0, 16:17, :], (16, WCOLS))
        coarse[1, 8:16, :] = jnp.ones((8, WCOLS), F32)

    @pl.when(gx == GX - 1)
    def _():
        coarse[0, 48:64, :] = jnp.broadcast_to(coarse[0, 47:48, :], (16, WCOLS))
        coarse[1, 48:56, :] = jnp.ones((8, WCOLS), F32)

    coarse_out[...] = coarse[:, 12 : 12 + HEAT_ROWS, :]

    p = sublanes((128, 128))
    q = lanes((128, 128))
    middle = 32 + q // 2
    beside = middle + 2 * (q % 2) - 1
    widen = jnp.where(p == middle, 0.75, 0.0) + jnp.where(p == beside, 0.25, 0.0)
    i = sublanes((EROWS, 64))
    c = lanes((EROWS, 64))
    middle = 8 + i // 2
    beside = middle + 2 * (i % 2) - 1
    raise_ = jnp.where(c == middle, 0.75, 0.0) + jnp.where(c == beside, 0.25, 0.0)
    warm = coarse[0]

    def columns(k):
        window = turn(warm, 32 - 64 * k, 1)[:, 0:128]
        return jnp.dot(window, widen, precision=HI, preferred_element_type=F32)

    lane64 = lanes((64, 128))
    tiles = [columns(k) for k in range(4)]
    tiles.append(jnp.where(lane64 < 64, columns(4), columns(-1)))
    for k in range(5):
        temp[k, 0:EROWS, :] = jnp.dot(raise_, tiles[k], precision=HI, preferred_element_type=F32)

    factor = -4.0 * LOG2E
    for rows, source in ((top, above), (low, below)):
        tile = source[0:16, :]
        for f in range(6):
            field[f, 4, rows, :] = join_sides(f, tile, 0, tile, 64)
        cw[1, rows, :] = factor * join_sides(6, tile, 0, tile, 64)
        cw[0, rows, :] = jnp.broadcast_to(factor * tile[:, 60:61], (HROW, 128))
    for f in range(6):
        field[f, 4, mid, :] = side[f]
    cw[1, mid, :] = factor * side[6]
    cw[0, mid, :] = factor * mark_rows(weights, 0, ROWS)

    lane = lanes((8, 128))
    first = gx * ROWS - HROW + BAND * sublanes((8, 128))
    rest = pl.ds(COLS, 128)
    col = gy * COLS + jnp.where(lane < 64, lane + COLS, lane - 128)
    inner_col = (col >= 1) & (col < GY * COLS)
    for t in range(BAND):
        row = first + t
        inner_row = (row >= 1) & (row < GX * ROWS)
        own_rate = cw[0, strip_of(t), :]
        for k in range(4):
            rate[t, :, pl.ds(128 * k, 128)] = own_rate
        rate[t, :, rest] = cw[1, strip_of(t), :]
        for k in range(5):
            warmth[t, :, pl.ds(128 * k, 128)] = (0.5 * EXPANSION) * temp[k, strip_of(t), :]
        for f in range(4):
            state[f, t, :, rest] = field[f, 4, strip_of(t), :]
        state[4, t, :, rest] = jnp.where(inner_row, field[4, 4, strip_of(t), :], 0.0)
        state[5, t, :, rest] = jnp.where(inner_col, field[5, 4, strip_of(t), :], 0.0)
    before = turn(warmth[BAND - 1], 1, 0)
    for t in range(BAND):
        own = warmth[t]
        tx[t] = own + before
        ty[t] = own + turn(own, 1, 1)
        before = own
    fetch.wait()

    keep = 1.0 - TIME_STEP * DAMPING

    def edge_x(t, a0, a1, o0, o1):
        open_x = a0 - o0 - tx[t]
        stretch = jnp.maximum(open_x, 0.0)
        spring = jnp.minimum(state[4, t], jnp.exp2(rate[t] * (stretch * stretch)))
        state[4, t] = spring
        return spring * open_x, spring * (a1 - o1)

    def substep(_, carry):
        a0, a1 = state[0, BAND - 1], state[1, BAND - 1]
        first_nx, first_ax = edge_x(0, state[0, 0], state[1, 0], turn(a0, 1, 0), turn(a1, 1, 0))
        next_nx, next_ax = turn(first_nx, -1, 0), turn(first_ax, -1, 0)
        for t in reversed(range(BAND)):
            open_y = a1 - turn(a1, 1, 1) - ty[t]
            stretch = jnp.maximum(open_y, 0.0)
            spring = jnp.minimum(state[5, t], jnp.exp2(rate[t] * (stretch * stretch)))
            state[5, t] = spring
            ny = spring * open_y
            ay = spring * (a0 - turn(a0, 1, 1))
            if t > 0:
                o0, o1 = state[0, t - 1], state[1, t - 1]
                nx, ax = edge_x(t, a0, a1, o0, o1)
            else:
                o0, o1 = a0, a1
                nx, ax = first_nx, first_ax
            force0 = (next_nx - nx) + (turn(ay, -1, 1) - ay)
            force1 = (next_ax - ax) + (turn(ny, -1, 1) - ny)
            next_nx, next_ax = nx, ax
            b0 = keep * state[2, t] + TIME_STEP * force0
            b1 = keep * state[3, t] + TIME_STEP * force1
            state[2, t] = b0
            state[3, t] = b1
            state[0, t] = a0 + TIME_STEP * b0
            state[1, t] = a1 + TIME_STEP * b1
            a0, a1 = o0, o1
        return carry

    lax.fori_loop(0, SUBSTEPS, substep, 0)
    for f in range(6):
        for t in range(BAND):
            for k in range(4):
                field[f, k, pl.ds(t, 8, stride=BAND), :] = state[f, t, :, pl.ds(128 * k, 128)]
        if f == 3:
            start_all(results[:-1])
    for b in range(10):
        rows = pl.ds(8 + 8 * b, 8)
        row = gx * ROWS - 8 + 8 * b + sublanes((8, 128))
        for k in range(4):
            cols = pl.ds(128 * k, 128)
            dx = jnp.where(row >= 1, 1.0 - field[4, k, rows, :], 0.0)
            dy = 1.0 - field[5, k, rows, :]
            if k == 0:
                dy = jnp.where(gy * COLS + lane >= 1, dy, 0.0)
            gap[k, pl.ds(8 * b, 8), :] = dx + dy
            if 1 <= b < 9:
                worn[0, pl.ds(8 * b - 8, 8), cols] = dx.astype(jnp.bfloat16)
                worn[1, pl.ds(8 * b - 8, 8), cols] = dy.astype(jnp.bfloat16)
    start_all(results[-1:])
    pairs = [
        gap[k, pl.ds(0, HEAT_ROWS, stride=2), :] + gap[k, pl.ds(1, HEAT_ROWS, stride=2), :]
        for k in range(4)
    ]
    for k in range(2):
        resist_out[:, pl.ds(128 * k, 128)] = jnp.dot(
            jnp.concatenate(pairs[2 * k : 2 * k + 2], axis=1),
            table[...],
            precision=HI,
            preferred_element_type=F32,
        )
    edge_out[...] = resist_out[:, 128:256]
    conduct = (1.0 + 0.5 * coarse[0, 12 : 12 + HEAT_ROWS, 0:CCOLS]) / (1.0 + resist_out[...])
    shape = (HEAT_ROWS, CCOLS)
    row = gx * CROWS - 4 + sublanes(shape)
    down = jnp.where((row >= 1) & (row < GX * CROWS), 0.5 * (conduct + turn(conduct, 1, 0)), 0.0)
    side = jnp.where(lanes(shape) >= 1, 0.5 * (conduct + turn(conduct, 1, 1)), 0.0)
    offsum = (down + turn(down, -1, 0) + side + turn(side, -1, 1))[4 : 4 + CROWS]
    capacity = coarse[1, 16:48, 0:CCOLS]
    top = jnp.max(offsum / (capacity + offsum), axis=(0, 1), keepdims=True)
    a = sublanes((8, CCOLS))
    c = lanes((8, CCOLS))
    border = jnp.where(sublanes((8, CROWS)) >= 6, top, 0.0)
    for k, value in enumerate((offsum, capacity, conduct[4 : 4 + CROWS])):
        pick = jnp.where(
            ((a == 2 * k) & (c == 0)) | ((a == 2 * k + 1) & (c == CCOLS - 1)), 1.0, 0.0
        )
        border += lax.dot_general(
            pick,
            value,
            (((1,), (1,)), ((), ())),
            precision=HI,
            preferred_element_type=F32,
        )
    for g in range(GX):
        border_tiles[g] = jnp.zeros((8, 128), F32)
        border_tiles[g, :, 0:CROWS] = border
    send = pltpu.make_async_copy(border_tiles, tops_out, sem.at[10])
    send.start()
    wait_all(results + [send])


def conductances(resist, from_left, coarse):
    gx = lax.axis_index("gx")
    gy = lax.axis_index("gy")
    shape = (HEAT_ROWS, WCOLS)
    lane = lanes((HEAT_ROWS, 128))
    rim = jnp.where(lane < 64, 0.0, from_left[...])
    wide = jnp.concatenate([resist[...], rim], axis=1)
    warm = coarse[0]
    conduct = (1.0 + 0.5 * warm) / (1.0 + wide)
    row = gx * CROWS - 4 + sublanes(shape)
    lane = lanes(shape)
    col = gy * CCOLS + jnp.where(lane < CCOLS + 64, lane, lane - WCOLS)
    down = jnp.where(
        (row >= 1) & (row < GX * CROWS), 0.5 * (conduct + turn(conduct, 1, 0)), 0.0
    )
    side = jnp.where(
        (col >= 1) & (col < GY * CCOLS), 0.5 * (conduct + turn(conduct, 1, 1)), 0.0
    )
    up = turn(down, -1, 0)
    far = turn(side, -1, 1)
    offsum = down + up + side + far
    return warm, down, up, side, far, offsum, coarse[1] + offsum


def solve_kernel(resist, from_left, coarse, tops, out):
    warm, down, up, side, far, _, diagonal = conductances(resist, from_left, coarse)
    inverse = 1.0 / diagonal

    def spread(x):
        return (
            down * turn(x, 1, 0) + up * turn(x, -1, 0) + side * turn(x, 1, 1) + far * turn(x, -1, 1)
        ) * inverse

    start = coarse[2] + (
        down * (turn(warm, 1, 0) - warm)
        + up * (turn(warm, -1, 0) - warm)
        + side * (turn(warm, 1, 1) - warm)
        + far * (turn(warm, -1, 1) - warm)
    )
    z = start * inverse
    y = z + spread(z)
    y2 = turn(spread(spread(y)), 4, 1)
    y = turn(y, 4, 1)
    group = lanes((8, 128)) // 32
    strip = []
    for h in range(2):
        tile = tops[4 * h]
        for k in range(1, 4):
            tile = jnp.where(group == k, turn(tops[4 * h + k], 32 * k, 1), tile)
        strip.append(tile)
    last_y, last_y2 = y[:, CCOLS:], turn(y2[:, CCOLS:], 64, 1)
    tail = jnp.where(lanes(last_y.shape) < 64, last_y, last_y2)
    for g in range(GY):
        rows = slice(4 + 2 * g, 6 + 2 * g)
        for h in range(2):
            cols = slice(128 * h, 128 * h + 128)
            out[g, 2 * h : 2 * h + 2, :] = y[rows, cols]
            out[g, 4 + 2 * h : 6 + 2 * h, :] = y2[rows, cols]
            out[g, 8 + 8 * h : 16 + 8 * h, :] = strip[h]
            out[g, 15 + 8 * h : 16 + 8 * h, :] = tail[4 + 2 * g + h : 5 + 2 * g + h]


def finish_kernel(recv, warm, out, wide, border):
    for g in range(GY):
        for k in range(7):
            for h in range(2):
                border[k, g : g + 1, pl.ds(128 * h, 128)] = recv[g, 8 + 8 * h + k : 9 + 8 * h + k, :]
    across = 0.5 * (turn(border[5], 1, 0) + border[4])
    across = jnp.where(sublanes((GY, CCOLS)) >= 1, across, 0.0)
    top = border[6]
    for k, face in ((0, across), (1, turn(across, -1, 0))):
        offsum = border[k] + face
        top = jnp.maximum(top, offsum / (border[2 + k] + offsum))
    top = jnp.max(top, axis=(0, 1), keepdims=True)
    square = top * top
    gain = 8.0 / (8.0 - 8.0 * square + square * square)
    near = gain * (1.0 - square)
    for g in range(GY):
        for h in range(2):
            wide[:, pl.ds(CCOLS * g + 128 * h, 128)] = (
                near * recv[g, 2 * h : 2 * h + 2, :] + gain * recv[g, 4 + 2 * h : 6 + 2 * h, :]
            )
    for h in range(2):
        tail = recv[GY - 1, 15 + 8 * h : 16 + 8 * h, :]
        wide[h : h + 1, pl.ds(CCOLS * GY, 128)] = near * tail + gain * turn(tail, 64, 1)
    out[...] = warm[...] + turn(wide[...], -4, 1)[:, : GY * CCOLS]


def vmem(count):
    return [pl.BlockSpec(memory_space=pltpu.VMEM)] * count


ANY = pl.BlockSpec(memory_space=pl.ANY)
FAR = pl.BlockSpec(memory_space=pltpu.MemorySpace.HBM)
PARAMS = pltpu.CompilerParams(vmem_limit_bytes=32 * 1024 * 1024)


def shaped(*shape, dtype=F32):
    return jax.ShapeDtypeStruct(shape, dtype)


def ahead(axis):
    count = lax.axis_size(axis)
    return [(i, (i + 1) % count) for i in range(count)]


def neighbours(value_up, value_down, axis):
    back = [(j, i) for i, j in ahead(axis)]
    return lax.ppermute(value_up, axis, ahead(axis)), lax.ppermute(value_down, axis, back)


def exchange(value, axis):
    return lax.all_to_all(value, axis, split_axis=0, concat_axis=0, tiled=True)


def per_device(u, v, d, marks, warm, cap, film, bath):
    far = [
        pltpu.with_memory_space_constraint(x, pltpu.MemorySpace.HBM)
        for x in (marks.reshape(ROWS // 8), u, v, d, warm, cap, film, bath)
    ]
    side = pltpu.VMEM((2, 2, ROWS, 128), F32)
    line = pltpu.VMEM((2, GY * CCOLS), F32)
    packed, weights = pl.pallas_call(
        pack_kernel,
        out_shape=(shaped(GY, CHUNK, 128), shaped(8, 128)),
        in_specs=[FAR] * 8,
        out_specs=tuple(vmem(2)),
        scratch_shapes=[pltpu.SMEM((ROWS // 8,), jnp.int32)]
        + [side, side, pltpu.VMEM((2, 2, ROWS, 128), jnp.int32)]
        + [line] * 4
        + [pltpu.VMEM((8, GY * CCOLS), F32), pltpu.SemaphoreType.DMA((11,))],
        compiler_params=PARAMS,
        name="pack",
    )(*far)
    recv = exchange(packed, "gy")
    up_rows, down_rows = pl.pallas_call(
        rows_kernel,
        out_shape=(shaped(6, 4, HROW, 128), shaped(6, 4, HROW, 128)),
        in_specs=vmem(1) + [FAR] * 3,
        out_specs=tuple(vmem(2)),
        scratch_shapes=[
            pltpu.VMEM((2, 2, HROW, COLS), jnp.int32),
            pltpu.SemaphoreType.DMA((18,)),
        ],
        compiler_params=PARAMS,
        name="rows",
    )(weights, *far[1:4])
    above_rows, below_rows = neighbours(up_rows, down_rows, "gx")
    up, down = pl.pallas_call(
        rim_kernel,
        out_shape=(shaped(CORNER, 128), shaped(CORNER, 128)),
        in_specs=vmem(2),
        out_specs=tuple(vmem(2)),
        compiler_params=PARAMS,
        name="rim",
    )(weights, recv)
    above, below = neighbours(up, down, "gx")
    state, side, coarse, table = pl.pallas_call(
        prep_kernel,
        out_shape=(
            shaped(6, BAND, 8, ECOLS),
            shaped(7, ROWS, 128),
            shaped(3, CROWS, WCOLS),
            shaped(256, 128),
        ),
        in_specs=vmem(1) + [ANY, ANY] + vmem(2) + [ANY, ANY],
        out_specs=tuple(vmem(4)),
        scratch_shapes=[
            pltpu.VMEM((6, 4, EROWS + 16, 128), F32),
            pltpu.SemaphoreType.DMA((10,)),
        ],
        compiler_params=PARAMS,
        name="prep",
    )(weights, u, v, d, recv, above_rows, below_rows)
    band = pltpu.VMEM((BAND, 8, ECOLS), F32)
    shift, speed, damage, resist, coarse, edge, tops = pl.pallas_call(
        plate_kernel,
        out_shape=(
            shaped(2, ROWS, COLS),
            shaped(2, ROWS, COLS),
            shaped(2, ROWS, COLS, dtype=jnp.bfloat16),
            shaped(HEAT_ROWS, CCOLS),
            shaped(3, HEAT_ROWS, WCOLS),
            shaped(HEAT_ROWS, 128),
            shaped(GX, 8, 128),
        ),
        in_specs=vmem(1) + [ANY] + vmem(5),
        out_specs=(ANY, ANY, ANY) + tuple(vmem(3)) + (ANY,),
        scratch_shapes=[
            pltpu.VMEM((6, 5, EROWS + 16, 128), F32),
            pltpu.VMEM((2, EROWS + 16, 128), F32),
            pltpu.VMEM((5, EROWS + 16, 128), F32),
            pltpu.VMEM((6, BAND, 8, ECOLS), F32),
            band,
            band,
            band,
            band,
            pltpu.VMEM((3, 64, WCOLS), F32),
            pltpu.VMEM((4, 2 * HEAT_ROWS + 8, 128), F32),
            pltpu.VMEM((2, ROWS, COLS), jnp.bfloat16),
            pltpu.VMEM((GX, 8, 128), F32),
            pltpu.SemaphoreType.DMA((11,)),
        ],
        compiler_params=PARAMS,
        name="plate",
    )(weights, state, side, coarse, table, above, below)
    from_left = lax.ppermute(edge, "gy", ahead("gy"))
    tops = exchange(tops, "gx")
    answer = pl.pallas_call(
        solve_kernel,
        out_shape=shaped(GY, 24, 128),
        in_specs=vmem(4),
        out_specs=vmem(1)[0],
        compiler_params=PARAMS,
        name="solve",
    )(resist, from_left, coarse, tops)
    answer = exchange(answer, "gy")
    warmth = pl.pallas_call(
        finish_kernel,
        out_shape=shaped(2, GY * CCOLS),
        in_specs=vmem(2),
        out_specs=vmem(1)[0],
        scratch_shapes=[pltpu.VMEM((2, GY * CCOLS + 128), F32), pltpu.VMEM((7, GY, CCOLS), F32)],
        compiler_params=PARAMS,
        name="finish",
    )(answer, warm)
    return shift, speed, damage, warmth


def solution(mesh):
    tile = P(None, "gx", "gy")
    line = P(("gx", "gy"), None)
    return jax.shard_map(
        per_device,
        mesh=mesh,
        in_specs=(tile, tile, tile, P("gx", "gy"), line, line, line, line),
        out_specs=(tile, tile, tile, line),
        check_vma=False,
    )
```
